1024 devices in a mesh: ctx: 64 (over x, z), head: 16 (over y, core).
Axes of the slice: x: 4, y: 8, z: 16, core: 2. Of those that a mesh axis runs over, the one named last changes fastest.
Arguments:
- queries: bfloat16 [8192, 4096], P('ctx', 'head'), may hold values from -4 to 4
- keys: bfloat16 [8192, 4096], P('ctx', 'head'), may hold values from -4 to 4
- values: bfloat16 [8192, 4096], P('ctx', 'head'), may hold values from -6 to 6
- outputs: bfloat16 [8192, 4096], P('ctx', 'head'), may hold values from -4 to 4
- grad_out: bfloat16 [8192, 4096], P(('ctx', 'head')), may hold values from -96 to 96
- log_norm: float32 [32, 8192], P('head', 'ctx'), may hold values from 6.5 to 7.5
- glob_keys: bfloat16 [256, 4096], P(None, 'head'), may hold values from -4 to 4
- glob_values: bfloat16 [256, 4096], P(None, 'head'), may hold values from -6 to 6
- key_lists: int32 [64, 6], replicated, may hold values from -1 to 63, as said below
Outputs:
- query_grads: bfloat16 [8192, 4096], P('ctx', 'head')
- key_grads: bfloat16 [8192, 4096], P('ctx', 'head')
- value_grads: bfloat16 [8192, 4096], P('ctx', 'head')
- glob_key_grads: float32 [256, 4096], P('ctx', 'head')
- glob_value_grads: float32 [256, 4096], P('ctx', 'head')
The draws below stay inside these ranges and needn't reach their ends.
Inputs may be any that keep to these rules, and one draw needn't show every extreme that they name: `key_lists`: row i holds i - 1, i, i + 1 (each -1 where that block lies outside 0 to 63) and then, for r = 1 to 3, one block of group (i + r * 16) mod 64, where group c holds blocks c * 1 to (c + 1) - 1.
All inputs are finite; a program needn't handle non-finite values.
Results may differ from the reference program's by a relative error of at most 0.0055.
Values may be sent and summed in bfloat16 or wider, within the bound.
No kernel may reach another device: no remote copies, remote signals or barrier semaphores. Data moves between devices by JAX's collectives and lax.ppermute only.
A program may use at most 32 MiB of HBM per device.

```python
import jax
import jax.numpy as jnp
from jax import lax

HEADS = 32
HEAD_DIM = 128
BLOCK = 128
GLOB = 256
RAND = 3
LIST = 6
BLK_DEV = 1
GROUPS = 64
STRIDE = 16
NB = 64
SEQ = 8192


def draw_key_lists(key, part):
    block_ids = jnp.arange(NB, dtype=jnp.int32)
    window = block_ids[:, None] + jnp.arange(-1, 2, dtype=jnp.int32)[None, :]
    window = jnp.where((window >= 0) & (window < NB), window, -1)
    group_ids = block_ids // BLK_DEV
    rounds = jnp.arange(1, RAND + 1, dtype=jnp.int32)
    target = (group_ids[:, None] + rounds[None, :] * STRIDE) % GROUPS
    within = jax.random.randint(key, (NB, RAND), 0, BLK_DEV, dtype=jnp.int32)
    return jnp.concatenate([window, target * BLK_DEV + within], axis=1).astype(jnp.int32)


def block_scale(stream_key, extent, shards, least, largest):
    gain, own = 1.0, jax.random.fold_in(stream_key, 6)
    for axis_at, blocks in shards:
        heights = jnp.exp(jax.random.uniform(jax.random.fold_in(own, axis_at), (blocks,), jnp.float32, least / len(shards), largest / len(shards)))
        gain = gain * jnp.repeat(heights, extent[axis_at] // blocks).reshape([-1 if axis == axis_at else 1 for axis in range(len(extent))])
    return gain


def normal_values(own_key, dims, deviation, limit, cuts=(), kind=jnp.bfloat16):
    drawn = jax.random.normal(own_key, dims, jnp.float32) * deviation
    if len(cuts) > 0:
        drawn = block_scale(own_key, dims, cuts, -0.22, 0.18) * drawn
    return jnp.clip(drawn, min=-limit, max=limit).astype(kind)


def setup_inputs(seed: int = 0) -> dict:
    splits = jax.random.split(jax.random.key(seed), 10)
    return {
        "queries": normal_values(splits[0], (SEQ, HEADS * HEAD_DIM), 0.5, 4.0, ((0, 64), (1, 16))),
        "keys": normal_values(splits[1], (SEQ, HEADS * HEAD_DIM), 1.0, 4.0, ((0, 64), (1, 16))),
        "values": normal_values(splits[2], (SEQ, HEADS * HEAD_DIM), 1.0, 6.0, ((0, 64), (1, 16))),
        "outputs": normal_values(splits[3], (SEQ, HEADS * HEAD_DIM), 0.3, 4.0, ((0, 64), (1, 16))),
        "grad_out": normal_values(splits[4], (SEQ, HEADS * HEAD_DIM), 16.0, 96.0, ((0, 1024),)),
        "log_norm": jnp.clip(6.5 + 1.0 * jax.random.uniform(splits[5], (HEADS, SEQ), jnp.float32) ** block_scale(splits[5], (HEADS, SEQ), ((0, 16), (1, 64)), -0.2, 0.2), 6.5, 7.5),
        "glob_keys": normal_values(splits[6], (GLOB, HEADS * HEAD_DIM), 1.0, 4.0, ((1, 16),)),
        "glob_values": normal_values(splits[7], (GLOB, HEADS * HEAD_DIM), 1.0, 6.0, ((1, 16),)),
        "key_lists": draw_key_lists(jax.random.fold_in(splits[9], 71), 0),
    }


def tile_grads(query_rows, grad_rows, norm_rows, delta_rows, key_rows, value_rows, keep_mask):
    att_scale = HEAD_DIM ** -0.5
    query_full = query_rows.astype(jnp.float32)
    grad_full = grad_rows.astype(jnp.float32)
    key_full = key_rows.astype(jnp.float32)
    value_full = value_rows.astype(jnp.float32)
    scores = jnp.einsum("nbd,nkd->nbk", query_full, key_full) * att_scale
    weights = jnp.exp(scores - norm_rows[:, :, None]) * keep_mask[:, None, :]
    dprobs = jnp.einsum("nbd,nkd->nbk", grad_full, value_full)
    dscores = weights * (dprobs - delta_rows[:, :, None])
    weights_low = lax.optimization_barrier(weights.astype(jnp.bfloat16)).astype(jnp.float32)
    dscores_low = lax.optimization_barrier(dscores.astype(jnp.bfloat16)).astype(jnp.float32)
    grad_values = jnp.einsum("nbk,nbd->nkd", weights_low, grad_full)
    grad_keys = jnp.einsum("nbk,nbd->nkd", dscores_low, query_full) * att_scale
    grad_queries = jnp.einsum("nbk,nkd->nbd", dscores_low, key_full) * att_scale
    return grad_queries, grad_keys, grad_values


def reference(queries, keys, values, outputs, grad_out, log_norm, glob_keys, glob_values, key_lists):
    num_blocks = key_lists.shape[0]
    live_mask = key_lists >= 0
    slot_ids = jnp.maximum(key_lists, 0).astype(jnp.int32)
    keep_all = jnp.concatenate([jnp.ones((num_blocks, GLOB), jnp.float32), jnp.repeat(live_mask.astype(jnp.float32), BLOCK, axis=1)], axis=1)

    def one_head(head_index):
        start = (head_index * HEAD_DIM).astype(jnp.int32)

        def head_cols(source):
            return lax.dynamic_slice_in_dim(source, start, HEAD_DIM, 1)

        def head_tiles(source):
            return head_cols(source).reshape(num_blocks, BLOCK, HEAD_DIM)

        query_tiles = head_tiles(queries)
        key_tiles = head_tiles(keys)
        value_tiles = head_tiles(values)
        grad_tiles = head_tiles(grad_out)
        output_tiles = head_tiles(outputs)
        glob_key_rows = head_cols(glob_keys)[None]
        glob_value_rows = head_cols(glob_values)[None]
        norm_tiles = lax.dynamic_index_in_dim(log_norm, head_index, 0, keepdims=False).reshape(num_blocks, BLOCK)
        delta_tiles = jnp.sum(grad_tiles.astype(jnp.float32) * output_tiles.astype(jnp.float32), axis=2)

        def visit(running, block_index):
            acc_keys, acc_values, acc_glob_keys, acc_glob_values = running
            list_row = lax.dynamic_index_in_dim(slot_ids, block_index, 0, keepdims=False)
            key_rows = jnp.concatenate([glob_key_rows, jnp.take(key_tiles, list_row, axis=0).reshape(1, LIST * BLOCK, HEAD_DIM)], axis=1)
            value_rows = jnp.concatenate([glob_value_rows, jnp.take(value_tiles, list_row, axis=0).reshape(1, LIST * BLOCK, HEAD_DIM)], axis=1)

            def pick(source):
                return lax.dynamic_slice_in_dim(source, block_index, 1, 0)

            grad_q, grad_k, grad_v = tile_grads(pick(query_tiles), pick(grad_tiles), pick(norm_tiles), pick(delta_tiles), key_rows, value_rows, pick(keep_all))
            acc_keys = acc_keys.at[list_row].add(grad_k[0, GLOB:].reshape(LIST, BLOCK, HEAD_DIM))
            acc_values = acc_values.at[list_row].add(grad_v[0, GLOB:].reshape(LIST, BLOCK, HEAD_DIM))
            acc_glob_keys = acc_glob_keys + grad_k[0, :GLOB]
            acc_glob_values = acc_glob_values + grad_v[0, :GLOB]
            return (acc_keys, acc_values, acc_glob_keys, acc_glob_values), grad_q[0].astype(jnp.bfloat16)

        zero_tiles = jnp.zeros((num_blocks, BLOCK, HEAD_DIM), jnp.float32)
        zero_glob = jnp.zeros((GLOB, HEAD_DIM), jnp.float32)
        running, dq_tiles = lax.scan(visit, (zero_tiles, zero_tiles, zero_glob, zero_glob), jnp.arange(num_blocks, dtype=jnp.int32))
        return dq_tiles, running[0].astype(jnp.bfloat16), running[1].astype(jnp.bfloat16), running[2], running[3]

    dq_all, dk_all, dv_all, gk_all, gv_all = lax.map(one_head, jnp.arange(HEADS, dtype=jnp.int32))

    def join_tokens(stacked):
        return jnp.transpose(stacked, (1, 2, 0, 3)).reshape(num_blocks * BLOCK, HEADS * HEAD_DIM)

    def join_glob(stacked):
        return jnp.transpose(stacked, (1, 0, 2)).reshape(GLOB, HEADS * HEAD_DIM)

    return join_tokens(dq_all), join_tokens(dk_all), join_tokens(dv_all), join_glob(gk_all), join_glob(gv_all)
```

```python
import jax
import jax.numpy as jnp
from jax import lax
from jax.experimental import pallas as pl
from jax.experimental.pallas import tpu as pltpu
from jax.sharding import Mesh
from jax.sharding import PartitionSpec as P

HEAD_DIM = 128
BLOCK = 128
GLOB = 256
RAND = 3
RING = RAND + 1
SCALE = HEAD_DIM ** (-0.5)
NORM_ROWS = 16
INTERPRET = False


def nt(lhs, rhs):
    return lax.dot_general(
        lhs, rhs, (((1,), (1,)), ((), ())), preferred_element_type=jnp.float32
    )


def nn(lhs, rhs):
    return lax.dot_general(
        lhs, rhs, (((1,), (0,)), ((), ())), preferred_element_type=jnp.float32
    )


def tn(lhs, rhs):
    return lax.dot_general(
        lhs, rhs, (((0,), (0,)), ((), ())), preferred_element_type=jnp.float32
    )


def prepare_body(q_ref, k_ref, v_ref, o_ref, norm_ref, go_ref, kv_ref, pack_ref, spread_ref):
    kv_ref[0:BLOCK] = k_ref[...]
    kv_ref[BLOCK : 2 * BLOCK] = v_ref[...]
    pack_ref[0:BLOCK] = k_ref[...]
    pack_ref[BLOCK : 2 * BLOCK] = v_ref[...]
    pack_ref[2 * BLOCK : 3 * BLOCK] = q_ref[...]
    pack_ref[3 * BLOCK : 4 * BLOCK] = o_ref[...]
    norm = jnp.concatenate([norm_ref[0:1, :], norm_ref[1:2, :]], axis=1)
    high = norm.astype(jnp.bfloat16).astype(jnp.float32)
    middle = (norm - high).astype(jnp.bfloat16).astype(jnp.float32)
    low = norm - high - middle
    rows = jnp.concatenate(
        [high, middle, low, jnp.zeros((NORM_ROWS - 3, norm.shape[1]), jnp.float32)], axis=0
    )
    pack_ref[4 * BLOCK : 4 * BLOCK + NORM_ROWS] = rows.astype(jnp.bfloat16)
    cols = spread_ref.shape[2]
    peers = spread_ref.shape[0] // RING
    for peer in range(peers):
        piece = go_ref[:, peer * cols : (peer + 1) * cols]
        for copy in range(RING):
            spread_ref[copy * peers + peer] = piece


def main_body(
    place_ref, q_ref, k_ref, v_ref, o_ref, norm_ref, far1_ref, far2_ref, far3_ref,
    left_ref, right_ref, go_ref, gk_ref, gv_ref,
    dq_ref, dk_ref, dv_ref, to_left_ref, to_right_ref, glob_ref,
):
    mine = place_ref[0]
    share = GLOB // RING
    far_refs = (far1_ref, far2_ref, far3_ref)
    share_at = pl.multiple_of(mine * share, share)
    ones = jnp.ones((8, HEAD_DIM), jnp.float32)
    for head in range(q_ref.shape[1] // HEAD_DIM):
        cols = slice(head * HEAD_DIM, (head + 1) * HEAD_DIM)

        def far_rows(part):
            return [ref[part * BLOCK : (part + 1) * BLOCK, cols] for ref in far_refs]

        far_norms = []
        for ref in far_refs:
            rows = ref[4 * BLOCK : 4 * BLOCK + NORM_ROWS, cols].astype(jnp.float32)
            far_norms.append(rows[0:1] + rows[1:2] + rows[2:3])
        norms = jnp.concatenate([norm_ref[head : head + 1, :]] + far_norms, axis=1)
        queries = jnp.concatenate([q_ref[:, cols]] + far_rows(2), axis=0)
        outputs = jnp.concatenate([o_ref[:, cols]] + far_rows(3), axis=0)
        grads = jnp.concatenate(
            [
                go_ref[pl.ds(pl.multiple_of(lax.rem(mine + hop, RING) * BLOCK, BLOCK), BLOCK), cols]
                for hop in range(RING)
            ],
            axis=0,
        )
        deltas = lax.dot_general(
            ones,
            grads.astype(jnp.float32) * outputs.astype(jnp.float32),
            (((1,), (1,)), ((), ())),
            precision=lax.Precision.HIGHEST,
            preferred_element_type=jnp.float32,
        )[0:1]
        own_q, own_g = queries[0:BLOCK], grads[0:BLOCK]

        key_rows = jnp.concatenate(
            [left_ref[0:BLOCK, cols], right_ref[0:BLOCK, cols], k_ref[:, cols]]
            + far_rows(0)
            + [gk_ref[:, cols]],
            axis=0,
        )
        value_rows = jnp.concatenate(
            [left_ref[BLOCK:, cols], right_ref[BLOCK:, cols], v_ref[:, cols]]
            + far_rows(1)
            + [gv_ref[:, cols]],
            axis=0,
        )
        weights = jnp.exp(nt(key_rows, own_q) * SCALE - norms[:, 0:BLOCK])
        dscores = weights * (nt(value_rows, own_g) - deltas[:, 0:BLOCK])
        dscores_low = dscores.astype(jnp.bfloat16)
        dq_ref[:, cols] = (tn(dscores_low, key_rows) * SCALE).astype(jnp.bfloat16)
        near = 2 * BLOCK
        near_dk = (nn(dscores_low[0:near], own_q) * SCALE).astype(jnp.bfloat16)
        near_dv = nn(weights[0:near].astype(jnp.bfloat16), own_g).astype(jnp.bfloat16)
        to_left_ref[0:BLOCK, cols] = near_dk[0:BLOCK]
        to_left_ref[BLOCK:, cols] = near_dv[0:BLOCK]
        to_right_ref[0:BLOCK, cols] = near_dk[BLOCK:]
        to_right_ref[BLOCK:, cols] = near_dv[BLOCK:]

        own_rows = jnp.concatenate([k_ref[:, cols], gk_ref[pl.ds(share_at, share), cols]], axis=0)
        own_values = jnp.concatenate([v_ref[:, cols], gv_ref[pl.ds(share_at, share), cols]], axis=0)
        weights = jnp.exp(nt(own_rows, queries) * SCALE - norms)
        dscores = weights * (nt(own_values, grads) - deltas)
        grad_k = nn(dscores.astype(jnp.bfloat16), queries) * SCALE
        grad_v = nn(weights.astype(jnp.bfloat16), grads)
        dk_ref[:, cols] = grad_k[0:BLOCK]
        dv_ref[:, cols] = grad_v[0:BLOCK]
        pieces = glob_ref.shape[0]
        rows = share // pieces
        for piece in range(pieces):
            at = BLOCK + piece * rows
            glob_ref[piece, :, cols] = jnp.concatenate(
                [grad_k[at : at + rows], grad_v[at : at + rows]], axis=0
            ).astype(jnp.bfloat16)


def finish_body(dk_ref, dv_ref, from_left_ref, from_right_ref, glob_ref, k_out, v_out, gk_out, gv_out):
    k_out[...] = (
        dk_ref[...]
        + from_left_ref[0:BLOCK].astype(jnp.float32)
        + from_right_ref[0:BLOCK].astype(jnp.float32)
    ).astype(jnp.bfloat16)
    v_out[...] = (
        dv_ref[...]
        + from_left_ref[BLOCK:].astype(jnp.float32)
        + from_right_ref[BLOCK:].astype(jnp.float32)
    ).astype(jnp.bfloat16)
    total = jnp.sum(glob_ref[...].astype(jnp.float32), axis=0)
    rows = gk_out.shape[0]
    gk_out[...] = total[0:rows]
    gv_out[...] = total[rows:]


def in_vmem(count):
    return [pl.BlockSpec(memory_space=pltpu.VMEM) for _ in range(count)]


def shards(queries, keys, values, outputs, grad_out, log_norm, glob_keys, glob_values, key_lists):
    cols = queries.shape[1]
    z_count = lax.axis_size("z")
    peers = lax.axis_size("head")
    ctx_count = RING * z_count
    bf16, f32 = jnp.bfloat16, jnp.float32
    shape = jax.ShapeDtypeStruct

    def to(value, by, wrap):
        pairs = [
            (i, (i + by) % ctx_count) for i in range(ctx_count) if wrap or 0 <= i + by < ctx_count
        ]
        return lax.ppermute(value, ("x", "z"), pairs)

    own_pair, pack, spread = pl.pallas_call(
        prepare_body,
        out_shape=(
            shape((2 * BLOCK, cols), bf16),
            shape((4 * BLOCK + NORM_ROWS, cols), bf16),
            shape((RING * peers, BLOCK // peers, cols), bf16),
        ),
        in_specs=in_vmem(6),
        out_specs=in_vmem(3),
        interpret=INTERPRET,
        name="prepare",
    )(queries, keys, values, outputs, log_norm, grad_out)
    incoming = lax.all_to_all(spread, ("x", "head"), split_axis=0, concat_axis=0, tiled=True)
    far = [to(pack, -(hop * z_count), True) for hop in range(1, RING)]
    left = to(own_pair, 1, False)
    right = to(own_pair, -1, False)
    place = lax.axis_index("x").astype(jnp.int32).reshape(1)
    share_rows = GLOB // ctx_count
    dq, dk, dv, to_left, to_right, glob = pl.pallas_call(
        main_body,
        out_shape=(
            shape((BLOCK, cols), bf16),
            shape((BLOCK, cols), f32),
            shape((BLOCK, cols), f32),
            shape((2 * BLOCK, cols), bf16),
            shape((2 * BLOCK, cols), bf16),
            shape((z_count, 2 * share_rows, cols), bf16),
        ),
        in_specs=[pl.BlockSpec(memory_space=pltpu.SMEM)] + in_vmem(13),
        out_specs=in_vmem(6),
        interpret=INTERPRET,
        name="tile_grads",
    )(
        place, queries, keys, values, outputs, log_norm, *far, left, right,
        incoming.reshape(RING * BLOCK, cols), glob_keys, glob_values,
    )
    glob_terms = lax.all_to_all(glob, "z", split_axis=0, concat_axis=0, tiled=True)
    from_right = to(to_left, -1, False)
    from_left = to(to_right, 1, False)
    dk_out, dv_out, gk_out, gv_out = pl.pallas_call(
        finish_body,
        out_shape=(
            shape((BLOCK, cols), bf16),
            shape((BLOCK, cols), bf16),
            shape((share_rows, cols), f32),
            shape((share_rows, cols), f32),
        ),
        in_specs=in_vmem(5),
        out_specs=in_vmem(4),
        interpret=INTERPRET,
        name="finish",
    )(dk, dv, from_left, from_right, glob_terms)
    return dq, dk_out, dv_out, gk_out, gv_out


def solution(mesh):
    ctx_count, head_count = mesh.shape["ctx"], mesh.shape["head"]
    grid = Mesh(
        mesh.devices.reshape(RING, ctx_count // RING, head_count), ("x", "z", "head")
    )
    ctx = ("x", "z")
    in_specs = (
        P(ctx, "head"),
        P(ctx, "head"),
        P(ctx, "head"),
        P(ctx, "head"),
        P((*ctx, "head"), None),
        P("head", ctx),
        P(None, "head"),
        P(None, "head"),
        P(),
    )
    out_specs = (P(ctx, "head"),) * 5
    return jax.shard_map(shards, mesh=grid, in_specs=in_specs, out_specs=out_specs, check_vma=False)
```

```python
import jax
import jax.numpy as jnp
from jax import lax
from jax.experimental import pallas as pl
from jax.experimental.pallas import tpu as pltpu
from jax.sharding import Mesh
from jax.sharding import PartitionSpec as P

HEAD_DIM = 128
BLOCK = 128
GLOB = 256
RAND = 3
RING = RAND + 1
SCALE = HEAD_DIM ** (-0.5)
QUERY_AT, GRAD_AT, TERM_AT = 0, BLOCK, 2 * BLOCK
QUERY_ROWS = TERM_AT + 16
KEY_AT, VALUE_AT = QUERY_ROWS, QUERY_ROWS + BLOCK
PACK_ROWS = QUERY_ROWS + 2 * BLOCK
INTERPRET = False


def nt(lhs, rhs):
    return lax.dot_general(
        lhs, rhs, (((1,), (1,)), ((), ())), preferred_element_type=jnp.float32
    )


def nn(lhs, rhs):
    return lax.dot_general(
        lhs, rhs, (((1,), (0,)), ((), ())), preferred_element_type=jnp.float32
    )


def tn(lhs, rhs):
    return lax.dot_general(
        lhs, rhs, (((0,), (0,)), ((), ())), preferred_element_type=jnp.float32
    )


def three_terms(value):
    high = value.astype(jnp.bfloat16).astype(jnp.float32)
    middle = (value - high).astype(jnp.bfloat16).astype(jnp.float32)
    return [high, middle, value - high - middle]


def norm_and_delta(rows):
    rows = rows.astype(jnp.float32)
    return rows[0:1] + rows[1:2] + rows[2:3], rows[3:4] + rows[4:5] + rows[5:6]


def split_body(go_ref, out_ref):
    cols = out_ref.shape[2]
    for peer in range(out_ref.shape[0]):
        out_ref[peer] = go_ref[:, peer * cols : (peer + 1) * cols]


def pack_body(go_ref, o_ref, k_ref, v_ref, q_ref, norm_ref, pack_ref, spread_ref):
    ones = jnp.ones((8, HEAD_DIM), jnp.float32)
    product = go_ref[...].astype(jnp.float32) * o_ref[...].astype(jnp.float32)
    deltas, norms = [], []
    for head in range(norm_ref.shape[0]):
        sums = lax.dot_general(
            ones,
            product[:, head * HEAD_DIM : (head + 1) * HEAD_DIM],
            (((1,), (1,)), ((), ())),
            precision=lax.Precision.HIGHEST,
            preferred_element_type=jnp.float32,
        )
        deltas.append(sums[0:1])
        norms.append(norm_ref[head : head + 1, :])
    terms = three_terms(jnp.concatenate(norms, axis=1)) + three_terms(jnp.concatenate(deltas, axis=1))
    pad = jnp.zeros((QUERY_ROWS - TERM_AT - len(terms), go_ref.shape[1]), jnp.float32)
    terms = jnp.concatenate(terms + [pad], axis=0).astype(jnp.bfloat16)
    for out in (pack_ref, *(spread_ref.at[peer] for peer in range(RING))):
        out[QUERY_AT:GRAD_AT] = q_ref[...]
        out[GRAD_AT:TERM_AT] = go_ref[...]
        out[TERM_AT:QUERY_ROWS] = terms
    pack_ref[KEY_AT:VALUE_AT] = k_ref[...]
    pack_ref[VALUE_AT:] = v_ref[...]


def key_side(keys, values, queries, grads, norms, deltas):
    weights = jnp.exp(nt(keys, queries) * SCALE - norms)
    dscores = weights * (nt(values, grads) - deltas)
    dscores_low = dscores.astype(jnp.bfloat16)
    grad_k = nn(dscores_low, queries) * SCALE
    grad_v = nn(weights.astype(jnp.bfloat16), grads)
    return grad_k, grad_v, dscores_low


def gathered(packs, cols):
    def rows(at):
        return jnp.concatenate([pack[at : at + BLOCK, cols] for pack in packs], axis=0)

    stats = [norm_and_delta(pack[TERM_AT:QUERY_ROWS, cols]) for pack in packs]
    norms, deltas = (jnp.concatenate(part, axis=1) for part in zip(*stats))
    return rows(QUERY_AT), rows(GRAD_AT), norms, deltas


def glob_body(place_ref, group_ref, gk_ref, gv_ref, out_ref):
    pieces = out_ref.shape[0]
    share = GLOB // RING
    share_at = pl.multiple_of(place_ref[0] * share, share)
    rows_each = share // pieces
    packs = [group_ref.at[member] for member in range(RING)]
    for head in range(gk_ref.shape[1] // HEAD_DIM):
        cols = slice(head * HEAD_DIM, (head + 1) * HEAD_DIM)
        grad_k, grad_v, _ = key_side(
            gk_ref[pl.ds(share_at, share), cols],
            gv_ref[pl.ds(share_at, share), cols],
            *gathered(packs, cols),
        )
        for piece in range(pieces):
            part = slice(piece * rows_each, (piece + 1) * rows_each)
            out_ref[piece, :, cols] = jnp.concatenate([grad_k[part], grad_v[part]], axis=0).astype(
                jnp.bfloat16
            )


def block_body(
    place_ref, group_ref, pack_ref, left_ref, right_ref, gk_ref, gv_ref,
    dq_ref, far1_ref, far2_ref, far3_ref, dk_ref, dv_ref,
):
    sides = [pack_ref, left_ref, right_ref]
    packs = sides + [group_ref.at[lax.rem(place_ref[0] + hop, RING)] for hop in range(1, RING)]
    for head in range(gk_ref.shape[1] // HEAD_DIM):
        cols = slice(head * HEAD_DIM, (head + 1) * HEAD_DIM)
        queries, grads, norms, deltas = gathered(packs, cols)
        own_q, own_g = queries[0:BLOCK], grads[0:BLOCK]
        keys = jnp.concatenate([ref[KEY_AT:VALUE_AT, cols] for ref in sides] + [gk_ref[:, cols]], axis=0)
        values = jnp.concatenate([ref[VALUE_AT:, cols] for ref in sides] + [gv_ref[:, cols]], axis=0)
        weights = jnp.exp(nt(keys, own_q) * SCALE - norms[:, 0:BLOCK])
        dscores = weights * (nt(values, own_g) - deltas[:, 0:BLOCK])
        dq_ref[:, cols] = tn(dscores.astype(jnp.bfloat16), keys) * SCALE
        own_k = keys[0:BLOCK]
        grad_k, grad_v, dscores_low = key_side(own_k, values[0:BLOCK], queries, grads, norms, deltas)
        dk_ref[:, cols] = grad_k.astype(jnp.bfloat16)
        dv_ref[:, cols] = grad_v.astype(jnp.bfloat16)
        far_dq = (tn(dscores_low[:, len(sides) * BLOCK :], own_k) * SCALE).astype(jnp.bfloat16)
        for hop, out_ref in enumerate((far1_ref, far2_ref, far3_ref)):
            out_ref[:, cols] = far_dq[hop * BLOCK : (hop + 1) * BLOCK]


def finish_body(dq_ref, far1_ref, far2_ref, far3_ref, terms_ref, out_ref, gk_ref, gv_ref):
    total = dq_ref[...]
    for ref in (far1_ref, far2_ref, far3_ref):
        total = total + ref[...].astype(jnp.float32)
    out_ref[...] = total.astype(jnp.bfloat16)
    terms = jnp.sum(terms_ref[...].astype(jnp.float32), axis=0)
    rows = gk_ref.shape[0]
    gk_ref[...] = terms[0:rows]
    gv_ref[...] = terms[rows:]


def in_vmem(count):
    return [pl.BlockSpec(memory_space=pltpu.VMEM) for _ in range(count)]


def near(value):
    return pltpu.with_memory_space_constraint(value, pltpu.VMEM)


def shards(queries, keys, values, outputs, grad_out, log_norm, glob_keys, glob_values, key_lists):
    cols = queries.shape[1]
    z_count = lax.axis_size("z")
    peers = lax.axis_size("head")
    ctx_count = RING * z_count
    share_rows = GLOB // ctx_count
    bf16, f32 = jnp.bfloat16, jnp.float32
    shape = jax.ShapeDtypeStruct
    place_spec = pl.BlockSpec(memory_space=pltpu.SMEM)
    place = lax.axis_index("x").astype(jnp.int32).reshape(1)

    def beside(value, by):
        pairs = [(i, i + by) for i in range(ctx_count) if 0 <= i + by < ctx_count]
        return lax.ppermute(value, ("x", "z"), pairs)

    def back(value, hop):
        pairs = [(i, (i + hop * z_count) % ctx_count) for i in range(ctx_count)]
        return lax.ppermute(value, ("x", "z"), pairs)

    def swap(value, axis):
        return lax.all_to_all(value, axis, split_axis=0, concat_axis=0, tiled=True)

    split = pl.pallas_call(
        split_body,
        out_shape=pltpu.VMEM((peers, BLOCK // peers, cols), bf16),
        in_specs=in_vmem(1),
        out_specs=in_vmem(1)[0],
        interpret=INTERPRET,
        name="split",
    )(grad_out)
    incoming = swap(split, "head").reshape(BLOCK, cols)
    pack, spread = pl.pallas_call(
        pack_body,
        out_shape=(
            pltpu.VMEM((PACK_ROWS, cols), bf16),
            pltpu.VMEM((RING, QUERY_ROWS, cols), bf16),
        ),
        in_specs=in_vmem(6),
        out_specs=in_vmem(2),
        interpret=INTERPRET,
        name="pack",
    )(near(incoming), near(outputs), near(keys), near(values), near(queries), log_norm)
    group = near(swap(spread, "x"))
    left = near(beside(pack, 1))
    right = near(beside(pack, -1))
    gk_near, gv_near = near(glob_keys), near(glob_values)
    glob = pl.pallas_call(
        glob_body,
        out_shape=pltpu.VMEM((z_count, 2 * share_rows, cols), bf16),
        in_specs=[place_spec] + in_vmem(3),
        out_specs=in_vmem(1)[0],
        interpret=INTERPRET,
        name="glob_grads",
    )(place, group, gk_near, gv_near)
    terms = near(swap(glob, "z"))
    dq, *far, dk, dv = pl.pallas_call(
        block_body,
        out_shape=(
            pltpu.VMEM((BLOCK, cols), f32),
            *(pltpu.VMEM((BLOCK, cols), bf16) for _ in range(RAND)),
            shape((BLOCK, cols), bf16),
            shape((BLOCK, cols), bf16),
        ),
        in_specs=[place_spec] + in_vmem(6),
        out_specs=in_vmem(6),
        interpret=INTERPRET,
        name="block_grads",
    )(place, group, near(pack), left, right, gk_near, gv_near)
    far = [near(back(part, hop)) for hop, part in enumerate(far, 1)]
    dq, gk, gv = pl.pallas_call(
        finish_body,
        out_shape=(
            shape((BLOCK, cols), bf16),
            shape((share_rows, cols), f32),
            shape((share_rows, cols), f32),
        ),
        in_specs=in_vmem(5),
        out_specs=in_vmem(3),
        interpret=INTERPRET,
        name="finish",
    )(near(dq), *far, terms)
    return dq, dk, dv, gk, gv


def solution(mesh):
    ctx_count, head_count = mesh.shape["ctx"], mesh.shape["head"]
    grid = Mesh(
        mesh.devices.reshape(RING, ctx_count // RING, head_count), ("x", "z", "head")
    )
    ctx = ("x", "z")
    in_specs = (
        P(ctx, "head"),
        P(ctx, "head"),
        P(ctx, "head"),
        P(ctx, "head"),
        P((*ctx, "head"), None),
        P("head", ctx),
        P(None, "head"),
        P(None, "head"),
        P(),
    )
    out_specs = (P(ctx, "head"),) * 5
    return jax.shard_map(shards, mesh=grid, in_specs=in_specs, out_specs=out_specs, check_vma=False)
```

```python
import jax
import jax.numpy as jnp
from jax import lax
from jax.experimental import pallas as pl
from jax.experimental.pallas import tpu as pltpu
from jax.sharding import Mesh
from jax.sharding import PartitionSpec as P

HEAD_DIM = 128
BLOCK = 128
GLOB = 256
RAND = 3
RING = RAND + 1
SCALE = HEAD_DIM ** (-0.5)
QUERY_AT, GRAD_AT, TERM_AT = 0, BLOCK, 2 * BLOCK
QUERY_ROWS = TERM_AT + 16
KEY_AT, VALUE_AT = QUERY_ROWS, QUERY_ROWS + BLOCK
PACK_ROWS = QUERY_ROWS + 2 * BLOCK
INTERPRET = False


def nt(lhs, rhs):
    return lax.dot_general(
        lhs, rhs, (((1,), (1,)), ((), ())), preferred_element_type=jnp.float32
    )


def nn(lhs, rhs):
    return lax.dot_general(
        lhs, rhs, (((1,), (0,)), ((), ())), preferred_element_type=jnp.float32
    )


def tn(lhs, rhs):
    return lax.dot_general(
        lhs, rhs, (((0,), (0,)), ((), ())), preferred_element_type=jnp.float32
    )


def three_terms(value):
    high = value.astype(jnp.bfloat16).astype(jnp.float32)
    middle = (value - high).astype(jnp.bfloat16).astype(jnp.float32)
    return [high, middle, value - high - middle]


def norm_and_delta(rows):
    rows = rows.astype(jnp.float32)
    return rows[0:1] + rows[1:2] + rows[2:3], rows[3:4] + rows[4:5] + rows[5:6]


def split_body(go_ref, out_ref):
    cols = out_ref.shape[2]
    for peer in range(out_ref.shape[0]):
        out_ref[peer] = go_ref[:, peer * cols : (peer + 1) * cols]


def pack_body(go_ref, o_ref, k_ref, v_ref, q_ref, norm_ref, pack_ref, spread_ref):
    ones = jnp.ones((8, HEAD_DIM), jnp.float32)
    product = go_ref[...].astype(jnp.float32) * o_ref[...].astype(jnp.float32)
    deltas, norms = [], []
    for head in range(norm_ref.shape[0]):
        sums = lax.dot_general(
            ones,
            product[:, head * HEAD_DIM : (head + 1) * HEAD_DIM],
            (((1,), (1,)), ((), ())),
            precision=lax.Precision.HIGHEST,
            preferred_element_type=jnp.float32,
        )
        deltas.append(sums[0:1])
        norms.append(norm_ref[head : head + 1, :])
    terms = three_terms(jnp.concatenate(norms, axis=1)) + three_terms(jnp.concatenate(deltas, axis=1))
    pad = jnp.zeros((QUERY_ROWS - TERM_AT - len(terms), go_ref.shape[1]), jnp.float32)
    terms = jnp.concatenate(terms + [pad], axis=0).astype(jnp.bfloat16)
    for out in (pack_ref, *(spread_ref.at[peer] for peer in range(RING))):
        out[QUERY_AT:GRAD_AT] = q_ref[...]
        out[GRAD_AT:TERM_AT] = go_ref[...]
        out[TERM_AT:QUERY_ROWS] = terms
    pack_ref[KEY_AT:VALUE_AT] = k_ref[...]
    pack_ref[VALUE_AT:] = v_ref[...]


def key_side(keys, values, queries, grads, norms, deltas):
    weights = jnp.exp(nt(keys, queries) * SCALE - norms)
    dscores = weights * (nt(values, grads) - deltas)
    dscores_low = dscores.astype(jnp.bfloat16)
    grad_k = nn(dscores_low, queries) * SCALE
    grad_v = nn(weights.astype(jnp.bfloat16), grads)
    return grad_k, grad_v, dscores_low


def gathered(packs, cols):
    def rows(at):
        return jnp.concatenate([pack[at : at + BLOCK, cols] for pack in packs], axis=0)

    stats = [norm_and_delta(pack[TERM_AT:QUERY_ROWS, cols]) for pack in packs]
    norms, deltas = (jnp.concatenate(part, axis=1) for part in zip(*stats))
    return rows(QUERY_AT), rows(GRAD_AT), norms, deltas


def glob_body(place_ref, group_ref, gk_ref, gv_ref, out_ref):
    pieces = out_ref.shape[0]
    share = GLOB // RING
    share_at = pl.multiple_of(place_ref[0] * share, share)
    rows_each = share // pieces
    packs = [group_ref.at[member] for member in range(RING)]
    for head in range(gk_ref.shape[1] // HEAD_DIM):
        cols = slice(head * HEAD_DIM, (head + 1) * HEAD_DIM)
        grad_k, grad_v, _ = key_side(
            gk_ref[pl.ds(share_at, share), cols],
            gv_ref[pl.ds(share_at, share), cols],
            *gathered(packs, cols),
        )
        for piece in range(pieces):
            part = slice(piece * rows_each, (piece + 1) * rows_each)
            out_ref[piece, :, cols] = jnp.concatenate([grad_k[part], grad_v[part]], axis=0).astype(
                jnp.bfloat16
            )


def query_side(keys, values, queries, grads, norms, deltas):
    weights = jnp.exp(nt(keys, queries) * SCALE - norms)
    dscores = weights * (nt(values, grads) - deltas)
    return tn(dscores.astype(jnp.bfloat16), keys) * SCALE


def own_body(pack_ref, gk_ref, gv_ref, dq_ref, copy_ref):
    copy_ref[...] = pack_ref[...]
    for head in range(gk_ref.shape[1] // HEAD_DIM):
        cols = slice(head * HEAD_DIM, (head + 1) * HEAD_DIM)
        keys = jnp.concatenate([pack_ref[KEY_AT:VALUE_AT, cols], gk_ref[:, cols]], axis=0)
        values = jnp.concatenate([pack_ref[VALUE_AT:, cols], gv_ref[:, cols]], axis=0)
        dq_ref[:, cols] = query_side(keys, values, *gathered([pack_ref], cols))


def block_body(
    place_ref, group_ref, pack_ref, left_ref, right_ref, own_dq_ref,
    dq_ref, far1_ref, far2_ref, far3_ref, dk_ref, dv_ref,
):
    sides = [pack_ref, left_ref, right_ref]
    packs = sides + [group_ref.at[lax.rem(place_ref[0] + hop, RING)] for hop in range(1, RING)]
    for head in range(own_dq_ref.shape[1] // HEAD_DIM):
        cols = slice(head * HEAD_DIM, (head + 1) * HEAD_DIM)
        queries, grads, norms, deltas = gathered(packs, cols)
        own_q, own_g = queries[0:BLOCK], grads[0:BLOCK]
        keys = jnp.concatenate([ref[KEY_AT:VALUE_AT, cols] for ref in sides[1:]], axis=0)
        values = jnp.concatenate([ref[VALUE_AT:, cols] for ref in sides[1:]], axis=0)
        dq_ref[:, cols] = own_dq_ref[:, cols] + query_side(
            keys, values, own_q, own_g, norms[:, 0:BLOCK], deltas[:, 0:BLOCK]
        )
        own_k, own_v = pack_ref[KEY_AT:VALUE_AT, cols], pack_ref[VALUE_AT:, cols]
        grad_k, grad_v, dscores_low = key_side(own_k, own_v, queries, grads, norms, deltas)
        dk_ref[:, cols] = grad_k.astype(jnp.bfloat16)
        dv_ref[:, cols] = grad_v.astype(jnp.bfloat16)
        far_dq = (tn(dscores_low[:, len(sides) * BLOCK :], own_k) * SCALE).astype(jnp.bfloat16)
        for hop, out_ref in enumerate((far1_ref, far2_ref, far3_ref)):
            out_ref[:, cols] = far_dq[hop * BLOCK : (hop + 1) * BLOCK]


def finish_body(dq_ref, far1_ref, far2_ref, far3_ref, terms_ref, out_ref, gk_ref, gv_ref):
    total = dq_ref[...]
    for ref in (far1_ref, far2_ref, far3_ref):
        total = total + ref[...].astype(jnp.float32)
    out_ref[...] = total.astype(jnp.bfloat16)
    terms = jnp.sum(terms_ref[...].astype(jnp.float32), axis=0)
    rows = gk_ref.shape[0]
    gk_ref[...] = terms[0:rows]
    gv_ref[...] = terms[rows:]


def in_vmem(count):
    return [pl.BlockSpec(memory_space=pltpu.VMEM) for _ in range(count)]


def near(value):
    return pltpu.with_memory_space_constraint(value, pltpu.VMEM)


def shards(queries, keys, values, outputs, grad_out, log_norm, glob_keys, glob_values, key_lists):
    cols = queries.shape[1]
    z_count = lax.axis_size("z")
    peers = lax.axis_size("head")
    ctx_count = RING * z_count
    share_rows = GLOB // ctx_count
    bf16, f32 = jnp.bfloat16, jnp.float32
    shape = jax.ShapeDtypeStruct
    place_spec = pl.BlockSpec(memory_space=pltpu.SMEM)
    place = lax.axis_index("x").astype(jnp.int32).reshape(1)

    def beside(value, by):
        pairs = [(i, i + by) for i in range(ctx_count) if 0 <= i + by < ctx_count]
        return lax.ppermute(value, ("x", "z"), pairs)

    def back(value, hop):
        pairs = [(i, (i + hop * z_count) % ctx_count) for i in range(ctx_count)]
        return lax.ppermute(value, ("x", "z"), pairs)

    def swap(value, axis):
        return lax.all_to_all(value, axis, split_axis=0, concat_axis=0, tiled=True)

    split = pl.pallas_call(
        split_body,
        out_shape=pltpu.VMEM((peers, BLOCK // peers, cols), bf16),
        in_specs=in_vmem(1),
        out_specs=in_vmem(1)[0],
        interpret=INTERPRET,
        name="split",
    )(grad_out)
    incoming = swap(split, "head").reshape(BLOCK, cols)
    pack, spread = pl.pallas_call(
        pack_body,
        out_shape=(
            pltpu.VMEM((PACK_ROWS, cols), bf16),
            pltpu.VMEM((RING, QUERY_ROWS, cols), bf16),
        ),
        in_specs=in_vmem(6),
        out_specs=in_vmem(2),
        interpret=INTERPRET,
        name="pack",
    )(near(incoming), near(outputs), near(keys), near(values), near(queries), log_norm)
    group = near(swap(spread, "x"))
    left = near(beside(pack, 1))
    gk_near, gv_near = near(glob_keys), near(glob_values)
    own_dq, pack_copy = pl.pallas_call(
        own_body,
        out_shape=(pltpu.VMEM((BLOCK, cols), f32), pltpu.VMEM((PACK_ROWS, cols), bf16)),
        in_specs=in_vmem(3),
        out_specs=in_vmem(2),
        interpret=INTERPRET,
        name="own_grads",
    )(near(pack), gk_near, gv_near)
    right = near(beside(pack_copy, -1))
    glob = pl.pallas_call(
        glob_body,
        out_shape=pltpu.VMEM((z_count, 2 * share_rows, cols), bf16),
        in_specs=[place_spec] + in_vmem(3),
        out_specs=in_vmem(1)[0],
        interpret=INTERPRET,
        name="glob_grads",
    )(place, group, gk_near, gv_near)
    terms = near(swap(glob, "z"))
    dq, *far, dk, dv = pl.pallas_call(
        block_body,
        out_shape=(
            pltpu.VMEM((BLOCK, cols), f32),
            *(pltpu.VMEM((BLOCK, cols), bf16) for _ in range(RAND)),
            shape((BLOCK, cols), bf16),
            shape((BLOCK, cols), bf16),
        ),
        in_specs=[place_spec] + in_vmem(5),
        out_specs=in_vmem(6),
        interpret=INTERPRET,
        name="block_grads",
    )(place, group, near(pack), left, right, near(own_dq))
    far = [near(back(part, hop)) for hop, part in enumerate(far, 1)]
    dq, gk, gv = pl.pallas_call(
        finish_body,
        out_shape=(
            shape((BLOCK, cols), bf16),
            shape((share_rows, cols), f32),
            shape((share_rows, cols), f32),
        ),
        in_specs=in_vmem(5),
        out_specs=in_vmem(3),
        interpret=INTERPRET,
        name="finish",
    )(near(dq), *far, terms)
    return dq, dk, dv, gk, gv


def solution(mesh):
    ctx_count, head_count = mesh.shape["ctx"], mesh.shape["head"]
    grid = Mesh(
        mesh.devices.reshape(RING, ctx_count // RING, head_count), ("x", "z", "head")
    )
    ctx = ("x", "z")
    in_specs = (
        P(ctx, "head"),
        P(ctx, "head"),
        P(ctx, "head"),
        P(ctx, "head"),
        P((*ctx, "head"), None),
        P("head", ctx),
        P(None, "head"),
        P(None, "head"),
        P(),
    )
    out_specs = (P(ctx, "head"),) * 5
    return jax.shard_map(shards, mesh=grid, in_specs=in_specs, out_specs=out_specs, check_vma=False)
```

```python
import jax
import jax.numpy as jnp
from jax import lax
from jax.experimental import pallas as pl
from jax.experimental.pallas import tpu as pltpu
from jax.sharding import Mesh
from jax.sharding import PartitionSpec as P

HEAD_DIM = 128
BLOCK = 128
GLOB = 256
RAND = 3
RING = RAND + 1
SCALE = HEAD_DIM ** (-0.5)
QUERY_AT, GRAD_AT, TERM_AT = 0, BLOCK, 2 * BLOCK
QUERY_ROWS = TERM_AT + 16
KEY_AT, VALUE_AT = QUERY_ROWS, QUERY_ROWS + BLOCK
PACK_ROWS = QUERY_ROWS + 2 * BLOCK
INTERPRET = False


def nt(lhs, rhs):
    return lax.dot_general(
        lhs, rhs, (((1,), (1,)), ((), ())), preferred_element_type=jnp.float32
    )


def nn(lhs, rhs):
    return lax.dot_general(
        lhs, rhs, (((1,), (0,)), ((), ())), preferred_element_type=jnp.float32
    )


def tn(lhs, rhs):
    return lax.dot_general(
        lhs, rhs, (((0,), (0,)), ((), ())), preferred_element_type=jnp.float32
    )


def three_terms(value):
    high = value.astype(jnp.bfloat16).astype(jnp.float32)
    middle = (value - high).astype(jnp.bfloat16).astype(jnp.float32)
    return [high, middle, value - high - middle]


def norm_and_delta(rows):
    rows = rows.astype(jnp.float32)
    return rows[0:1] + rows[1:2] + rows[2:3], rows[3:4] + rows[4:5] + rows[5:6]


def pack_body(go_ref, o_ref, q_ref, norm_ref, own_ref, spread_ref, norm_buf, sems):
    def send(part, source, at):
        rows = pl.ds(at, source.shape[0])
        return [
            pltpu.make_async_copy(source, spread_ref.at[peer, rows], sems.at[part * RING + peer])
            for peer in range(RING)
        ]

    load = pltpu.make_async_copy(norm_ref, norm_buf, sems.at[3 * RING])
    load.start()
    copies = send(0, q_ref, QUERY_AT) + send(1, go_ref, GRAD_AT)
    for copy in copies:
        copy.start()
    own_ref[QUERY_AT:GRAD_AT] = q_ref[...]
    own_ref[GRAD_AT:TERM_AT] = go_ref[...]
    ones = jnp.ones((8, HEAD_DIM), jnp.float32)
    product = go_ref[...].astype(jnp.float32) * o_ref[...].astype(jnp.float32)
    deltas = []
    for at in range(0, go_ref.shape[1], HEAD_DIM):
        sums = lax.dot_general(
            ones,
            product[:, at : at + HEAD_DIM],
            (((1,), (1,)), ((), ())),
            precision=lax.Precision.HIGHEST,
            preferred_element_type=jnp.float32,
        )
        deltas.append(sums[0:1])
    load.wait()
    norms = [norm_buf[head : head + 1, :] for head in range(norm_buf.shape[0])]
    terms = three_terms(jnp.concatenate(norms, axis=1)) + three_terms(jnp.concatenate(deltas, axis=1))
    pad = jnp.zeros((QUERY_ROWS - TERM_AT - len(terms), go_ref.shape[1]), jnp.float32)
    own_ref[TERM_AT:QUERY_ROWS] = jnp.concatenate(terms + [pad], axis=0).astype(jnp.bfloat16)
    last = send(2, own_ref.at[pl.ds(TERM_AT, QUERY_ROWS - TERM_AT)], TERM_AT)
    for copy in last:
        copy.start()
    for copy in copies + last:
        copy.wait()


def key_side(keys, values, queries, grads, norms, deltas):
    weights = jnp.exp(nt(keys, queries) * SCALE - norms)
    dscores = weights * (nt(values, grads) - deltas)
    dscores_low = dscores.astype(jnp.bfloat16)
    grad_k = nn(dscores_low, queries) * SCALE
    grad_v = nn(weights.astype(jnp.bfloat16), grads)
    return grad_k, grad_v, dscores_low


def gathered(packs, cols):
    def rows(at):
        return jnp.concatenate([pack[at : at + BLOCK, cols] for pack in packs], axis=0)

    stats = [norm_and_delta(pack[TERM_AT:QUERY_ROWS, cols]) for pack in packs]
    norms, deltas = (jnp.concatenate(part, axis=1) for part in zip(*stats))
    return rows(QUERY_AT), rows(GRAD_AT), norms, deltas


def glob_body(place_ref, group_ref, gk_ref, gv_ref, out_ref):
    pieces = out_ref.shape[0]
    share = GLOB // RING
    share_at = pl.multiple_of(place_ref[0] * share, share)
    rows_each = share // pieces
    packs = [group_ref.at[member] for member in range(RING)]
    for head in range(gk_ref.shape[1] // HEAD_DIM):
        cols = slice(head * HEAD_DIM, (head + 1) * HEAD_DIM)
        grad_k, grad_v, _ = key_side(
            gk_ref[pl.ds(share_at, share), cols],
            gv_ref[pl.ds(share_at, share), cols],
            *gathered(packs, cols),
        )
        for piece in range(pieces):
            part = slice(piece * rows_each, (piece + 1) * rows_each)
            out_ref[piece, :, cols] = jnp.concatenate([grad_k[part], grad_v[part]], axis=0).astype(
                jnp.bfloat16
            )


def query_side(keys, values, queries, grads, norms, deltas):
    weights = jnp.exp(nt(keys, queries) * SCALE - norms)
    dscores = weights * (nt(values, grads) - deltas)
    return tn(dscores.astype(jnp.bfloat16), keys) * SCALE


def whole_body(own_ref, k_ref, v_ref, pack_ref):
    pack_ref[0:QUERY_ROWS] = own_ref[...]
    pack_ref[KEY_AT:VALUE_AT] = k_ref[...]
    pack_ref[VALUE_AT:] = v_ref[...]


def own_body(pack_ref, gk_ref, gv_ref, dq_ref, copy_ref):
    copy_ref[...] = pack_ref[...]
    for head in range(gk_ref.shape[1] // HEAD_DIM):
        cols = slice(head * HEAD_DIM, (head + 1) * HEAD_DIM)
        keys = jnp.concatenate([pack_ref[KEY_AT:VALUE_AT, cols], gk_ref[:, cols]], axis=0)
        values = jnp.concatenate([pack_ref[VALUE_AT:, cols], gv_ref[:, cols]], axis=0)
        dq_ref[:, cols] = query_side(keys, values, *gathered([pack_ref], cols))


def far_body(
    place_ref, group_ref, pack_ref, far1_ref, far2_ref, far3_ref, dk_ref, dv_ref
):
    packs = [group_ref.at[lax.rem(place_ref[0] + hop, RING)] for hop in range(1, RING)]
    for head in range(dk_ref.shape[1] // HEAD_DIM):
        cols = slice(head * HEAD_DIM, (head + 1) * HEAD_DIM)
        own_k, own_v = pack_ref[KEY_AT:VALUE_AT, cols], pack_ref[VALUE_AT:, cols]
        grad_k, grad_v, dscores_low = key_side(own_k, own_v, *gathered(packs, cols))
        dk_ref[:, cols] = grad_k
        dv_ref[:, cols] = grad_v
        far_dq = (tn(dscores_low, own_k) * SCALE).astype(jnp.bfloat16)
        for hop, out_ref in enumerate((far1_ref, far2_ref, far3_ref)):
            out_ref[:, cols] = far_dq[hop * BLOCK : (hop + 1) * BLOCK]


def near_body(
    pack_ref, left_ref, right_ref, own_dq_ref, far_dk_ref, far_dv_ref, dq_ref, dk_ref, dv_ref
):
    packs = [pack_ref, left_ref, right_ref]
    for head in range(dq_ref.shape[1] // HEAD_DIM):
        cols = slice(head * HEAD_DIM, (head + 1) * HEAD_DIM)
        queries, grads, norms, deltas = gathered(packs, cols)
        keys = jnp.concatenate([ref[KEY_AT:VALUE_AT, cols] for ref in packs[1:]], axis=0)
        values = jnp.concatenate([ref[VALUE_AT:, cols] for ref in packs[1:]], axis=0)
        dq_ref[:, cols] = own_dq_ref[:, cols] + query_side(
            keys, values, queries[0:BLOCK], grads[0:BLOCK], norms[:, 0:BLOCK], deltas[:, 0:BLOCK]
        )
        grad_k, grad_v, _ = key_side(
            pack_ref[KEY_AT:VALUE_AT, cols], pack_ref[VALUE_AT:, cols], queries, grads, norms, deltas
        )
        dk_ref[:, cols] = (far_dk_ref[:, cols] + grad_k).astype(jnp.bfloat16)
        dv_ref[:, cols] = (far_dv_ref[:, cols] + grad_v).astype(jnp.bfloat16)


def finish_body(dq_ref, far1_ref, far2_ref, far3_ref, terms_ref, out_ref, gk_ref, gv_ref):
    total = dq_ref[...]
    for ref in (far1_ref, far2_ref, far3_ref):
        total = total + ref[...].astype(jnp.float32)
    out_ref[...] = total.astype(jnp.bfloat16)
    terms = jnp.sum(terms_ref[...].astype(jnp.float32), axis=0)
    rows = gk_ref.shape[0]
    gk_ref[...] = terms[0:rows]
    gv_ref[...] = terms[rows:]


def in_vmem(count):
    return [pl.BlockSpec(memory_space=pltpu.VMEM) for _ in range(count)]


def near(value):
    return pltpu.with_memory_space_constraint(value, pltpu.VMEM)


def shards(queries, keys, values, outputs, grad_out, log_norm, glob_keys, glob_values, key_lists):
    cols = queries.shape[1]
    z_count = lax.axis_size("z")
    peers = lax.axis_size("head")
    ctx_count = RING * z_count
    share_rows = GLOB // ctx_count
    bf16, f32 = jnp.bfloat16, jnp.float32
    shape = jax.ShapeDtypeStruct
    place_spec = pl.BlockSpec(memory_space=pltpu.SMEM)
    place = lax.axis_index("x").astype(jnp.int32).reshape(1)

    def beside(value, by):
        pairs = [(i, i + by) for i in range(ctx_count) if 0 <= i + by < ctx_count]
        return lax.ppermute(value, ("x", "z"), pairs)

    def back(value, hop):
        pairs = [(i, (i + hop * z_count) % ctx_count) for i in range(ctx_count)]
        return lax.ppermute(value, ("x", "z"), pairs)

    def swap(value, axis):
        return lax.all_to_all(value, axis, split_axis=0, concat_axis=0, tiled=True)

    split = grad_out.reshape(BLOCK // peers, peers, cols).transpose(1, 0, 2)
    incoming = swap(split, "head").reshape(BLOCK, cols)
    own_rows, spread = pl.pallas_call(
        pack_body,
        out_shape=(
            pltpu.VMEM((QUERY_ROWS, cols), bf16),
            shape((RING, QUERY_ROWS, cols), bf16),
        ),
        in_specs=in_vmem(3) + [pl.BlockSpec(memory_space=pl.ANY)],
        out_specs=[pl.BlockSpec(memory_space=pltpu.VMEM), pl.BlockSpec(memory_space=pl.ANY)],
        scratch_shapes=[
            pltpu.VMEM(log_norm.shape, f32),
            pltpu.SemaphoreType.DMA((3 * RING + 1,)),
        ],
        interpret=INTERPRET,
        name="pack",
    )(near(incoming), near(outputs), near(queries), log_norm)
    group = near(swap(spread, "x"))
    gk_near, gv_near = near(glob_keys), near(glob_values)
    pack = pl.pallas_call(
        whole_body,
        out_shape=pltpu.VMEM((PACK_ROWS, cols), bf16),
        in_specs=in_vmem(3),
        out_specs=in_vmem(1)[0],
        interpret=INTERPRET,
        name="whole_pack",
    )(near(own_rows), near(keys), near(values))
    left = near(beside(pack, 1))
    own_dq, pack_copy = pl.pallas_call(
        own_body,
        out_shape=(pltpu.VMEM((BLOCK, cols), f32), pltpu.VMEM((PACK_ROWS, cols), bf16)),
        in_specs=in_vmem(3),
        out_specs=in_vmem(2),
        interpret=INTERPRET,
        name="own_grads",
    )(near(pack), gk_near, gv_near)
    right = near(beside(pack_copy, -1))
    glob = pl.pallas_call(
        glob_body,
        out_shape=pltpu.VMEM((z_count, 2 * share_rows, cols), bf16),
        in_specs=[place_spec] + in_vmem(3),
        out_specs=in_vmem(1)[0],
        interpret=INTERPRET,
        name="glob_grads",
    )(place, group, gk_near, gv_near)
    terms = near(swap(glob, "z"))
    *far, far_dk, far_dv = pl.pallas_call(
        far_body,
        out_shape=(
            *(pltpu.VMEM((BLOCK, cols), bf16) for _ in range(RAND)),
            pltpu.VMEM((BLOCK, cols), f32),
            pltpu.VMEM((BLOCK, cols), f32),
        ),
        in_specs=[place_spec] + in_vmem(2),
        out_specs=in_vmem(5),
        interpret=INTERPRET,
        name="far_grads",
    )(place, group, near(pack))
    far = [near(back(part, hop)) for hop, part in enumerate(far, 1)]
    dq, dk, dv = pl.pallas_call(
        near_body,
        out_shape=(
            pltpu.VMEM((BLOCK, cols), f32),
            shape((BLOCK, cols), bf16),
            shape((BLOCK, cols), bf16),
        ),
        in_specs=in_vmem(6),
        out_specs=in_vmem(3),
        interpret=INTERPRET,
        name="near_grads",
    )(near(pack), left, right, near(own_dq), near(far_dk), near(far_dv))
    dq, gk, gv = pl.pallas_call(
        finish_body,
        out_shape=(
            shape((BLOCK, cols), bf16),
            shape((share_rows, cols), f32),
            shape((share_rows, cols), f32),
        ),
        in_specs=in_vmem(5),
        out_specs=in_vmem(3),
        interpret=INTERPRET,
        name="finish",
    )(near(dq), *far, terms)
    return dq, dk, dv, gk, gv


def solution(mesh):
    ctx_count, head_count = mesh.shape["ctx"], mesh.shape["head"]
    grid = Mesh(
        mesh.devices.reshape(RING, ctx_count // RING, head_count), ("x", "z", "head")
    )
    ctx = ("x", "z")
    in_specs = (
        P(ctx, "head"),
        P(ctx, "head"),
        P(ctx, "head"),
        P(ctx, "head"),
        P((*ctx, "head"), None),
        P("head", ctx),
        P(None, "head"),
        P(None, "head"),
        P(),
    )
    out_specs = (P(ctx, "head"),) * 5
    return jax.shard_map(shards, mesh=grid, in_specs=in_specs, out_specs=out_specs, check_vma=False)
```

```python
import jax
import jax.numpy as jnp
from jax import lax
from jax.experimental import pallas as pl
from jax.experimental.pallas import tpu as pltpu
from jax.sharding import Mesh
from jax.sharding import PartitionSpec as P

HEAD_DIM = 128
BLOCK = 128
GLOB = 256
RAND = 3
RING = RAND + 1
SCALE = HEAD_DIM ** (-0.5)
QUERY_AT, GRAD_AT, TERM_AT = 0, BLOCK, 2 * BLOCK
QUERY_ROWS = TERM_AT + 16
KEY_AT, VALUE_AT = QUERY_ROWS, QUERY_ROWS + BLOCK
PACK_ROWS = QUERY_ROWS + 2 * BLOCK
INTERPRET = False


def nt(lhs, rhs):
    return lax.dot_general(
        lhs, rhs, (((1,), (1,)), ((), ())), preferred_element_type=jnp.float32
    )


def nn(lhs, rhs):
    return lax.dot_general(
        lhs, rhs, (((1,), (0,)), ((), ())), preferred_element_type=jnp.float32
    )


def tn(lhs, rhs):
    return lax.dot_general(
        lhs, rhs, (((0,), (0,)), ((), ())), preferred_element_type=jnp.float32
    )


def three_terms(value):
    high = value.astype(jnp.bfloat16).astype(jnp.float32)
    middle = (value - high).astype(jnp.bfloat16).astype(jnp.float32)
    return [high, middle, value - high - middle]


def norm_and_delta(rows):
    rows = rows.astype(jnp.float32)
    return rows[0:1] + rows[1:2] + rows[2:3], rows[3:4] + rows[4:5] + rows[5:6]


def pack_body(go_ref, o_ref, q_ref, norm_ref, own_ref, spread_ref, norm_buf, sems):
    def send(part, source, at):
        rows = pl.ds(at, source.shape[0])
        return [
            pltpu.make_async_copy(source, spread_ref.at[peer, rows], sems.at[part * RING + peer])
            for peer in range(RING)
        ]

    load = pltpu.make_async_copy(norm_ref, norm_buf, sems.at[3 * RING])
    load.start()
    copies = send(0, q_ref, QUERY_AT) + send(1, go_ref, GRAD_AT)
    for copy in copies:
        copy.start()
    own_ref[QUERY_AT:GRAD_AT] = q_ref[...]
    own_ref[GRAD_AT:TERM_AT] = go_ref[...]
    ones = jnp.ones((8, HEAD_DIM), jnp.float32)
    product = go_ref[...].astype(jnp.float32) * o_ref[...].astype(jnp.float32)
    deltas = []
    for at in range(0, go_ref.shape[1], HEAD_DIM):
        sums = lax.dot_general(
            ones,
            product[:, at : at + HEAD_DIM],
            (((1,), (1,)), ((), ())),
            precision=lax.Precision.HIGHEST,
            preferred_element_type=jnp.float32,
        )
        deltas.append(sums[0:1])
    load.wait()
    norms = [norm_buf[head : head + 1, :] for head in range(norm_buf.shape[0])]
    terms = three_terms(jnp.concatenate(norms, axis=1)) + three_terms(jnp.concatenate(deltas, axis=1))
    pad = jnp.zeros((QUERY_ROWS - TERM_AT - len(terms), go_ref.shape[1]), jnp.float32)
    own_ref[TERM_AT:QUERY_ROWS] = jnp.concatenate(terms + [pad], axis=0).astype(jnp.bfloat16)
    last = send(2, own_ref.at[pl.ds(TERM_AT, QUERY_ROWS - TERM_AT)], TERM_AT)
    for copy in last:
        copy.start()
    for copy in copies + last:
        copy.wait()


def key_side(keys, values, queries, grads, norms, deltas):
    weights = jnp.exp(nt(keys, queries) * SCALE - norms)
    dscores = weights * (nt(values, grads) - deltas)
    dscores_low = dscores.astype(jnp.bfloat16)
    grad_k = nn(dscores_low, queries) * SCALE
    grad_v = nn(weights.astype(jnp.bfloat16), grads)
    return grad_k, grad_v, dscores_low


def gathered(packs, cols):
    def rows(at):
        return jnp.concatenate([pack[at : at + BLOCK, cols] for pack in packs], axis=0)

    stats = [norm_and_delta(pack[TERM_AT:QUERY_ROWS, cols]) for pack in packs]
    norms, deltas = (jnp.concatenate(part, axis=1) for part in zip(*stats))
    return rows(QUERY_AT), rows(GRAD_AT), norms, deltas


def glob_body(place_ref, group_ref, gk_ref, gv_ref, out_ref):
    pieces = out_ref.shape[0]
    share = GLOB // RING
    share_at = pl.multiple_of(place_ref[0] * share, share)
    rows_each = share // pieces
    packs = [group_ref.at[member] for member in range(RING)]
    for head in range(gk_ref.shape[1] // HEAD_DIM):
        cols = slice(head * HEAD_DIM, (head + 1) * HEAD_DIM)
        grad_k, grad_v, _ = key_side(
            gk_ref[pl.ds(share_at, share), cols],
            gv_ref[pl.ds(share_at, share), cols],
            *gathered(packs, cols),
        )
        for piece in range(pieces):
            part = slice(piece * rows_each, (piece + 1) * rows_each)
            out_ref[piece, :, cols] = jnp.concatenate([grad_k[part], grad_v[part]], axis=0).astype(
                jnp.bfloat16
            )


def query_side(keys, values, queries, grads, norms, deltas):
    weights = jnp.exp(nt(keys, queries) * SCALE - norms)
    dscores = weights * (nt(values, grads) - deltas)
    return tn(dscores.astype(jnp.bfloat16), keys) * SCALE


def pair_body(k_ref, v_ref, out_ref):
    out_ref[0:BLOCK] = k_ref[...]
    out_ref[BLOCK:] = v_ref[...]


def gate_body(spread_ref, before_ref, out_ref):
    del spread_ref, before_ref, out_ref


def whole_body(own_ref, k_ref, v_ref, pack_ref):
    pack_ref[0:QUERY_ROWS] = own_ref[...]
    pack_ref[KEY_AT:VALUE_AT] = k_ref[...]
    pack_ref[VALUE_AT:] = v_ref[...]


def own_body(pack_ref, before_ref, gk_ref, gv_ref, dq_ref, copy_ref):
    copy_ref[...] = pack_ref[...]
    for head in range(gk_ref.shape[1] // HEAD_DIM):
        cols = slice(head * HEAD_DIM, (head + 1) * HEAD_DIM)
        keys = jnp.concatenate(
            [pack_ref[KEY_AT:VALUE_AT, cols], before_ref[0:BLOCK, cols], gk_ref[:, cols]], axis=0
        )
        values = jnp.concatenate(
            [pack_ref[VALUE_AT:, cols], before_ref[BLOCK:, cols], gv_ref[:, cols]], axis=0
        )
        dq_ref[:, cols] = query_side(keys, values, *gathered([pack_ref], cols))


def far_body(
    place_ref, group_ref, pack_ref, far2_ref, far3_ref, dk_ref, dv_ref
):
    packs = [group_ref.at[lax.rem(place_ref[0] + hop, RING)] for hop in (2, 3, 1)]
    for head in range(dk_ref.shape[1] // HEAD_DIM):
        cols = slice(head * HEAD_DIM, (head + 1) * HEAD_DIM)
        own_k, own_v = pack_ref[KEY_AT:VALUE_AT, cols], pack_ref[VALUE_AT:, cols]
        grad_k, grad_v, dscores_low = key_side(own_k, own_v, *gathered(packs, cols))
        dk_ref[:, cols] = grad_k
        dv_ref[:, cols] = grad_v
        far_dq = (tn(dscores_low[:, 0 : 2 * BLOCK], own_k) * SCALE).astype(jnp.bfloat16)
        far2_ref[:, cols] = far_dq[0:BLOCK]
        far3_ref[:, cols] = far_dq[BLOCK:]


def near_body(
    pack_ref, left_ref, right_ref, own_dq_ref, far_dk_ref, far_dv_ref, dq_ref, dk_ref, dv_ref
):
    packs = [pack_ref, left_ref, right_ref]
    for head in range(dq_ref.shape[1] // HEAD_DIM):
        cols = slice(head * HEAD_DIM, (head + 1) * HEAD_DIM)
        queries, grads, norms, deltas = gathered(packs, cols)
        keys = jnp.concatenate([ref[KEY_AT:VALUE_AT, cols] for ref in packs[1:]], axis=0)
        values = jnp.concatenate([ref[VALUE_AT:, cols] for ref in packs[1:]], axis=0)
        dq_ref[:, cols] = own_dq_ref[:, cols] + query_side(
            keys, values, queries[0:BLOCK], grads[0:BLOCK], norms[:, 0:BLOCK], deltas[:, 0:BLOCK]
        )
        grad_k, grad_v, _ = key_side(
            pack_ref[KEY_AT:VALUE_AT, cols], pack_ref[VALUE_AT:, cols], queries, grads, norms, deltas
        )
        dk_ref[:, cols] = (far_dk_ref[:, cols] + grad_k).astype(jnp.bfloat16)
        dv_ref[:, cols] = (far_dv_ref[:, cols] + grad_v).astype(jnp.bfloat16)


def finish_body(dq_ref, far2_ref, far3_ref, terms_ref, out_ref, gk_ref, gv_ref):
    total = dq_ref[...]
    for ref in (far2_ref, far3_ref):
        total = total + ref[...].astype(jnp.float32)
    out_ref[...] = total.astype(jnp.bfloat16)
    terms = jnp.sum(terms_ref[...].astype(jnp.float32), axis=0)
    rows = gk_ref.shape[0]
    gk_ref[...] = terms[0:rows]
    gv_ref[...] = terms[rows:]


def in_vmem(count):
    return [pl.BlockSpec(memory_space=pltpu.VMEM) for _ in range(count)]


def near(value):
    return pltpu.with_memory_space_constraint(value, pltpu.VMEM)


def shards(queries, keys, values, outputs, grad_out, log_norm, glob_keys, glob_values, key_lists):
    cols = queries.shape[1]
    z_count = lax.axis_size("z")
    peers = lax.axis_size("head")
    ctx_count = RING * z_count
    share_rows = GLOB // ctx_count
    bf16, f32 = jnp.bfloat16, jnp.float32
    shape = jax.ShapeDtypeStruct
    place_spec = pl.BlockSpec(memory_space=pltpu.SMEM)
    place = lax.axis_index("x").astype(jnp.int32).reshape(1)

    def beside(value, by):
        pairs = [(i, i + by) for i in range(ctx_count) if 0 <= i + by < ctx_count]
        return lax.ppermute(value, ("x", "z"), pairs)

    def back(value, hop):
        pairs = [(i, (i + hop * z_count) % ctx_count) for i in range(ctx_count)]
        return lax.ppermute(value, ("x", "z"), pairs)

    def swap(value, axis):
        return lax.all_to_all(value, axis, split_axis=0, concat_axis=0, tiled=True)

    split = grad_out.reshape(BLOCK // peers, peers, cols).transpose(1, 0, 2)
    incoming = swap(split, "head").reshape(BLOCK, cols)
    pair = pl.pallas_call(
        pair_body,
        out_shape=pltpu.VMEM((2 * BLOCK, cols), bf16),
        in_specs=in_vmem(2),
        out_specs=in_vmem(1)[0],
        interpret=INTERPRET,
        name="pair",
    )(keys, values)
    before = near(back(pair, 1))
    own_rows, spread = pl.pallas_call(
        pack_body,
        out_shape=(
            pltpu.VMEM((QUERY_ROWS, cols), bf16),
            shape((RING, QUERY_ROWS, cols), bf16),
        ),
        in_specs=in_vmem(3) + [pl.BlockSpec(memory_space=pl.ANY)],
        out_specs=[pl.BlockSpec(memory_space=pltpu.VMEM), pl.BlockSpec(memory_space=pl.ANY)],
        scratch_shapes=[
            pltpu.VMEM(log_norm.shape, f32),
            pltpu.SemaphoreType.DMA((3 * RING + 1,)),
        ],
        interpret=INTERPRET,
        cost_estimate=pl.CostEstimate(flops=1000000000, transcendentals=0, bytes_accessed=0),
        name="pack",
    )(near(incoming), near(outputs), near(queries), log_norm)
    anywhere = pl.BlockSpec(memory_space=pl.ANY)
    spread = pl.pallas_call(
        gate_body,
        out_shape=shape(spread.shape, bf16),
        in_specs=[anywhere, pl.BlockSpec(memory_space=pltpu.VMEM)],
        out_specs=anywhere,
        input_output_aliases={0: 0},
        interpret=INTERPRET,
        name="gate",
    )(spread, before)
    group = near(swap(spread, "x"))
    gk_near, gv_near = near(glob_keys), near(glob_values)
    pack = pl.pallas_call(
        whole_body,
        out_shape=pltpu.VMEM((PACK_ROWS, cols), bf16),
        in_specs=in_vmem(3),
        out_specs=in_vmem(1)[0],
        interpret=INTERPRET,
        name="whole_pack",
    )(near(own_rows), near(keys), near(values))
    left = near(beside(pack, 1))
    own_dq, pack_copy = pl.pallas_call(
        own_body,
        out_shape=(pltpu.VMEM((BLOCK, cols), f32), pltpu.VMEM((PACK_ROWS, cols), bf16)),
        in_specs=in_vmem(4),
        out_specs=in_vmem(2),
        interpret=INTERPRET,
        name="own_grads",
    )(near(pack), before, gk_near, gv_near)
    right = near(beside(pack_copy, -1))
    glob = pl.pallas_call(
        glob_body,
        out_shape=pltpu.VMEM((z_count, 2 * share_rows, cols), bf16),
        in_specs=[place_spec] + in_vmem(3),
        out_specs=in_vmem(1)[0],
        interpret=INTERPRET,
        name="glob_grads",
    )(place, group, gk_near, gv_near)
    terms = near(swap(glob, "z"))
    *far, far_dk, far_dv = pl.pallas_call(
        far_body,
        out_shape=(
            pltpu.VMEM((BLOCK, cols), bf16),
            pltpu.VMEM((BLOCK, cols), bf16),
            pltpu.VMEM((BLOCK, cols), f32),
            pltpu.VMEM((BLOCK, cols), f32),
        ),
        in_specs=[place_spec] + in_vmem(2),
        out_specs=in_vmem(4),
        interpret=INTERPRET,
        name="far_grads",
    )(place, group, near(pack))
    far = [near(back(part, hop)) for part, hop in zip(far, (2, 3))]
    dq, dk, dv = pl.pallas_call(
        near_body,
        out_shape=(
            pltpu.VMEM((BLOCK, cols), f32),
            shape((BLOCK, cols), bf16),
            shape((BLOCK, cols), bf16),
        ),
        in_specs=in_vmem(6),
        out_specs=in_vmem(3),
        interpret=INTERPRET,
        name="near_grads",
    )(near(pack), left, right, near(own_dq), near(far_dk), near(far_dv))
    dq, gk, gv = pl.pallas_call(
        finish_body,
        out_shape=(
            shape((BLOCK, cols), bf16),
            shape((share_rows, cols), f32),
            shape((share_rows, cols), f32),
        ),
        in_specs=in_vmem(4),
        out_specs=in_vmem(3),
        interpret=INTERPRET,
        name="finish",
    )(near(dq), *far, terms)
    return dq, dk, dv, gk, gv


def solution(mesh):
    ctx_count, head_count = mesh.shape["ctx"], mesh.shape["head"]
    grid = Mesh(
        mesh.devices.reshape(RING, ctx_count // RING, head_count), ("x", "z", "head")
    )
    ctx = ("x", "z")
    in_specs = (
        P(ctx, "head"),
        P(ctx, "head"),
        P(ctx, "head"),
        P(ctx, "head"),
        P((*ctx, "head"), None),
        P("head", ctx),
        P(None, "head"),
        P(None, "head"),
        P(),
    )
    out_specs = (P(ctx, "head"),) * 5
    return jax.shard_map(shards, mesh=grid, in_specs=in_specs, out_specs=out_specs, check_vma=False)
```

```python
import jax
import jax.numpy as jnp
from jax import lax
from jax.experimental import pallas as pl
from jax.experimental.pallas import tpu as pltpu
from jax.sharding import Mesh
from jax.sharding import PartitionSpec as P

HEAD_DIM = 128
BLOCK = 128
GLOB = 256
RAND = 3
RING = RAND + 1
SCALE = HEAD_DIM ** (-0.5)
QUERY_AT, GRAD_AT, TERM_AT = 0, BLOCK, 2 * BLOCK
QUERY_ROWS = TERM_AT + 16
KEY_AT, VALUE_AT = QUERY_ROWS, QUERY_ROWS + BLOCK
PACK_ROWS = QUERY_ROWS + 2 * BLOCK
INTERPRET = False


def nt(lhs, rhs):
    return lax.dot_general(
        lhs, rhs, (((1,), (1,)), ((), ())), preferred_element_type=jnp.float32
    )


def nn(lhs, rhs):
    return lax.dot_general(
        lhs, rhs, (((1,), (0,)), ((), ())), preferred_element_type=jnp.float32
    )


def tn(lhs, rhs):
    return lax.dot_general(
        lhs, rhs, (((0,), (0,)), ((), ())), preferred_element_type=jnp.float32
    )


def three_terms(value):
    high = value.astype(jnp.bfloat16).astype(jnp.float32)
    middle = (value - high).astype(jnp.bfloat16).astype(jnp.float32)
    return [high, middle, value - high - middle]


def norm_and_delta(rows):
    rows = rows.astype(jnp.float32)
    return rows[0:1] + rows[1:2] + rows[2:3], rows[3:4] + rows[4:5] + rows[5:6]


def pack_body(go_ref, o_ref, q_ref, norm_ref, own_ref, spread_ref, norm_buf, sems):
    def send(part, source, at):
        rows = pl.ds(at, source.shape[0])
        return [
            pltpu.make_async_copy(source, spread_ref.at[peer, rows], sems.at[part * RING + peer])
            for peer in range(RING)
        ]

    load = pltpu.make_async_copy(norm_ref, norm_buf, sems.at[3 * RING])
    load.start()
    copies = send(0, q_ref, QUERY_AT) + send(1, go_ref, GRAD_AT)
    for copy in copies:
        copy.start()
    own_ref[QUERY_AT:GRAD_AT] = q_ref[...]
    own_ref[GRAD_AT:TERM_AT] = go_ref[...]
    ones = jnp.ones((8, HEAD_DIM), jnp.float32)
    product = go_ref[...].astype(jnp.float32) * o_ref[...].astype(jnp.float32)
    deltas = []
    for at in range(0, go_ref.shape[1], HEAD_DIM):
        sums = lax.dot_general(
            ones,
            product[:, at : at + HEAD_DIM],
            (((1,), (1,)), ((), ())),
            precision=lax.Precision.HIGHEST,
            preferred_element_type=jnp.float32,
        )
        deltas.append(sums[0:1])
    load.wait()
    norms = [norm_buf[head : head + 1, :] for head in range(norm_buf.shape[0])]
    terms = three_terms(jnp.concatenate(norms, axis=1)) + three_terms(jnp.concatenate(deltas, axis=1))
    pad = jnp.zeros((QUERY_ROWS - TERM_AT - len(terms), go_ref.shape[1]), jnp.float32)
    own_ref[TERM_AT:QUERY_ROWS] = jnp.concatenate(terms + [pad], axis=0).astype(jnp.bfloat16)
    last = send(2, own_ref.at[pl.ds(TERM_AT, QUERY_ROWS - TERM_AT)], TERM_AT)
    for copy in last:
        copy.start()
    for copy in copies + last:
        copy.wait()


def key_side(keys, values, queries, grads, norms, deltas):
    weights = jnp.exp(nt(keys, queries) * SCALE - norms)
    dscores = weights * (nt(values, grads) - deltas)
    dscores_low = dscores.astype(jnp.bfloat16)
    grad_k = nn(dscores_low, queries) * SCALE
    grad_v = nn(weights.astype(jnp.bfloat16), grads)
    return grad_k, grad_v, dscores_low


def gathered(packs, cols):
    def rows(at):
        return jnp.concatenate([pack[at : at + BLOCK, cols] for pack in packs], axis=0)

    stats = [norm_and_delta(pack[TERM_AT:QUERY_ROWS, cols]) for pack in packs]
    norms, deltas = (jnp.concatenate(part, axis=1) for part in zip(*stats))
    return rows(QUERY_AT), rows(GRAD_AT), norms, deltas


def glob_body(place_ref, group_ref, gk_ref, gv_ref, out_ref):
    pieces = out_ref.shape[0]
    share = GLOB // RING
    share_at = pl.multiple_of(place_ref[0] * share, share)
    rows_each = share // pieces
    packs = [group_ref.at[member] for member in range(RING)]
    for head in range(gk_ref.shape[1] // HEAD_DIM):
        cols = slice(head * HEAD_DIM, (head + 1) * HEAD_DIM)
        grad_k, grad_v, _ = key_side(
            gk_ref[pl.ds(share_at, share), cols],
            gv_ref[pl.ds(share_at, share), cols],
            *gathered(packs, cols),
        )
        for piece in range(pieces):
            part = slice(piece * rows_each, (piece + 1) * rows_each)
            out_ref[piece, :, cols] = jnp.concatenate([grad_k[part], grad_v[part]], axis=0).astype(
                jnp.bfloat16
            )


def query_side(keys, values, queries, grads, norms, deltas):
    weights = jnp.exp(nt(keys, queries) * SCALE - norms)
    dscores = weights * (nt(values, grads) - deltas)
    return tn(dscores.astype(jnp.bfloat16), keys) * SCALE


def pair_body(k_ref, v_ref, gk_ref, gv_ref, out_ref, gk_out, gv_out):
    gk_out[...] = gk_ref[...]
    gv_out[...] = gv_ref[...]
    out_ref[0:BLOCK] = k_ref[...]
    out_ref[BLOCK:] = v_ref[...]


def whole_body(own_ref, k_ref, v_ref, before_ref, pack_ref):
    del before_ref
    pack_ref[0:QUERY_ROWS] = own_ref[...]
    pack_ref[KEY_AT:VALUE_AT] = k_ref[...]
    pack_ref[VALUE_AT:] = v_ref[...]


def own_body(pack_ref, before_ref, gk_ref, gv_ref, dq_ref, copy_ref):
    copy_ref[...] = pack_ref[...]
    for head in range(gk_ref.shape[1] // HEAD_DIM):
        cols = slice(head * HEAD_DIM, (head + 1) * HEAD_DIM)
        keys = jnp.concatenate(
            [pack_ref[KEY_AT:VALUE_AT, cols], before_ref[0:BLOCK, cols], gk_ref[:, cols]], axis=0
        )
        values = jnp.concatenate(
            [pack_ref[VALUE_AT:, cols], before_ref[BLOCK:, cols], gv_ref[:, cols]], axis=0
        )
        dq_ref[:, cols] = query_side(keys, values, *gathered([pack_ref], cols))


def far_body(
    place_ref, group_ref, pack_ref, far2_ref, far3_ref, dk_ref, dv_ref
):
    packs = [group_ref.at[lax.rem(place_ref[0] + hop, RING)] for hop in (2, 3, 1)]
    for head in range(dk_ref.shape[1] // HEAD_DIM):
        cols = slice(head * HEAD_DIM, (head + 1) * HEAD_DIM)
        own_k, own_v = pack_ref[KEY_AT:VALUE_AT, cols], pack_ref[VALUE_AT:, cols]
        grad_k, grad_v, dscores_low = key_side(own_k, own_v, *gathered(packs, cols))
        dk_ref[:, cols] = grad_k
        dv_ref[:, cols] = grad_v
        far_dq = (tn(dscores_low[:, 0 : 2 * BLOCK], own_k) * SCALE).astype(jnp.bfloat16)
        far2_ref[:, cols] = far_dq[0:BLOCK]
        far3_ref[:, cols] = far_dq[BLOCK:]


def near_body(
    pack_ref, left_ref, right_ref, own_dq_ref, far_dk_ref, far_dv_ref, dq_ref, dk_ref, dv_ref
):
    packs = [pack_ref, left_ref, right_ref]
    for head in range(dq_ref.shape[1] // HEAD_DIM):
        cols = slice(head * HEAD_DIM, (head + 1) * HEAD_DIM)
        queries, grads, norms, deltas = gathered(packs, cols)
        keys = jnp.concatenate([ref[KEY_AT:VALUE_AT, cols] for ref in packs[1:]], axis=0)
        values = jnp.concatenate([ref[VALUE_AT:, cols] for ref in packs[1:]], axis=0)
        dq_ref[:, cols] = own_dq_ref[:, cols] + query_side(
            keys, values, queries[0:BLOCK], grads[0:BLOCK], norms[:, 0:BLOCK], deltas[:, 0:BLOCK]
        )
        grad_k, grad_v, _ = key_side(
            pack_ref[KEY_AT:VALUE_AT, cols], pack_ref[VALUE_AT:, cols], queries, grads, norms, deltas
        )
        dk_ref[:, cols] = (far_dk_ref[:, cols] + grad_k).astype(jnp.bfloat16)
        dv_ref[:, cols] = (far_dv_ref[:, cols] + grad_v).astype(jnp.bfloat16)


def finish_body(dq_ref, far2_ref, far3_ref, terms_ref, out_ref, gk_ref, gv_ref):
    total = dq_ref[...]
    for ref in (far2_ref, far3_ref):
        total = total + ref[...].astype(jnp.float32)
    out_ref[...] = total.astype(jnp.bfloat16)
    terms = jnp.sum(terms_ref[...].astype(jnp.float32), axis=0)
    rows = gk_ref.shape[0]
    gk_ref[...] = terms[0:rows]
    gv_ref[...] = terms[rows:]


def in_vmem(count):
    return [pl.BlockSpec(memory_space=pltpu.VMEM) for _ in range(count)]


def near(value):
    return pltpu.with_memory_space_constraint(value, pltpu.VMEM)


def shards(queries, keys, values, outputs, grad_out, log_norm, glob_keys, glob_values, key_lists):
    cols = queries.shape[1]
    z_count = lax.axis_size("z")
    peers = lax.axis_size("head")
    ctx_count = RING * z_count
    share_rows = GLOB // ctx_count
    bf16, f32 = jnp.bfloat16, jnp.float32
    shape = jax.ShapeDtypeStruct
    place_spec = pl.BlockSpec(memory_space=pltpu.SMEM)
    place = lax.axis_index("x").astype(jnp.int32).reshape(1)

    def beside(value, by):
        pairs = [(i, i + by) for i in range(ctx_count) if 0 <= i + by < ctx_count]
        return lax.ppermute(value, ("x", "z"), pairs)

    def back(value, hop):
        pairs = [(i, (i + hop * z_count) % ctx_count) for i in range(ctx_count)]
        return lax.ppermute(value, ("x", "z"), pairs)

    def swap(value, axis):
        return lax.all_to_all(value, axis, split_axis=0, concat_axis=0, tiled=True)

    split = grad_out.reshape(BLOCK // peers, peers, cols).transpose(1, 0, 2)
    incoming = swap(split, "head").reshape(BLOCK, cols)
    pair, gk_near, gv_near = pl.pallas_call(
        pair_body,
        out_shape=(
            pltpu.VMEM((2 * BLOCK, cols), bf16),
            pltpu.VMEM((GLOB, cols), bf16),
            pltpu.VMEM((GLOB, cols), bf16),
        ),
        in_specs=in_vmem(4),
        out_specs=in_vmem(3),
        interpret=INTERPRET,
        name="pair",
    )(keys, values, glob_keys, glob_values)
    gk_near, gv_near = near(gk_near), near(gv_near)
    before = near(back(pair, 1))
    own_rows, spread = pl.pallas_call(
        pack_body,
        out_shape=(
            pltpu.VMEM((QUERY_ROWS, cols), bf16),
            shape((RING, QUERY_ROWS, cols), bf16),
        ),
        in_specs=in_vmem(3) + [pl.BlockSpec(memory_space=pl.ANY)],
        out_specs=[pl.BlockSpec(memory_space=pltpu.VMEM), pl.BlockSpec(memory_space=pl.ANY)],
        scratch_shapes=[
            pltpu.VMEM(log_norm.shape, f32),
            pltpu.SemaphoreType.DMA((3 * RING + 1,)),
        ],
        interpret=INTERPRET,
        cost_estimate=pl.CostEstimate(flops=1000000000, transcendentals=0, bytes_accessed=0),
        name="pack",
    )(near(incoming), near(outputs), near(queries), log_norm)
    group = near(swap(spread, "x"))
    pack = pl.pallas_call(
        whole_body,
        out_shape=pltpu.VMEM((PACK_ROWS, cols), bf16),
        in_specs=in_vmem(4),
        out_specs=in_vmem(1)[0],
        interpret=INTERPRET,
        cost_estimate=pl.CostEstimate(flops=5000000000, transcendentals=0, bytes_accessed=0),
        name="whole_pack",
    )(near(own_rows), near(keys), near(values), before)
    right = near(beside(pack, -1))
    own_dq, pack_copy = pl.pallas_call(
        own_body,
        out_shape=(pltpu.VMEM((BLOCK, cols), f32), pltpu.VMEM((PACK_ROWS, cols), bf16)),
        in_specs=in_vmem(4),
        out_specs=in_vmem(2),
        interpret=INTERPRET,
        name="own_grads",
    )(near(pack), before, gk_near, gv_near)
    left = near(beside(pack_copy, 1))
    glob = pl.pallas_call(
        glob_body,
        out_shape=pltpu.VMEM((z_count, 2 * share_rows, cols), bf16),
        in_specs=[place_spec] + in_vmem(3),
        out_specs=in_vmem(1)[0],
        interpret=INTERPRET,
        name="glob_grads",
    )(place, group, gk_near, gv_near)
    terms = near(swap(glob, "z"))
    *far, far_dk, far_dv = pl.pallas_call(
        far_body,
        out_shape=(
            pltpu.VMEM((BLOCK, cols), bf16),
            pltpu.VMEM((BLOCK, cols), bf16),
            pltpu.VMEM((BLOCK, cols), f32),
            pltpu.VMEM((BLOCK, cols), f32),
        ),
        in_specs=[place_spec] + in_vmem(2),
        out_specs=in_vmem(4),
        interpret=INTERPRET,
        name="far_grads",
    )(place, group, near(pack))
    far = [near(back(part, hop)) for part, hop in zip(far, (2, 3))]
    dq, dk, dv = pl.pallas_call(
        near_body,
        out_shape=(
            pltpu.VMEM((BLOCK, cols), f32),
            shape((BLOCK, cols), bf16),
            shape((BLOCK, cols), bf16),
        ),
        in_specs=in_vmem(6),
        out_specs=in_vmem(3),
        interpret=INTERPRET,
        name="near_grads",
    )(near(pack), left, right, near(own_dq), near(far_dk), near(far_dv))
    dq, gk, gv = pl.pallas_call(
        finish_body,
        out_shape=(
            shape((BLOCK, cols), bf16),
            shape((share_rows, cols), f32),
            shape((share_rows, cols), f32),
        ),
        in_specs=in_vmem(4),
        out_specs=in_vmem(3),
        interpret=INTERPRET,
        name="finish",
    )(near(dq), *far, terms)
    return dq, dk, dv, gk, gv


def solution(mesh):
    ctx_count, head_count = mesh.shape["ctx"], mesh.shape["head"]
    grid = Mesh(
        mesh.devices.reshape(RING, ctx_count // RING, head_count), ("x", "z", "head")
    )
    ctx = ("x", "z")
    in_specs = (
        P(ctx, "head"),
        P(ctx, "head"),
        P(ctx, "head"),
        P(ctx, "head"),
        P((*ctx, "head"), None),
        P("head", ctx),
        P(None, "head"),
        P(None, "head"),
        P(),
    )
    out_specs = (P(ctx, "head"),) * 5
    return jax.shard_map(shards, mesh=grid, in_specs=in_specs, out_specs=out_specs, check_vma=False)
```

```python
import jax
import jax.numpy as jnp
from jax import lax
from jax.experimental import pallas as pl
from jax.experimental.pallas import tpu as pltpu
from jax.sharding import Mesh
from jax.sharding import PartitionSpec as P

HEAD_DIM = 128
BLOCK = 128
GLOB = 256
RAND = 3
RING = RAND + 1
SCALE = HEAD_DIM ** (-0.5)
QUERY_AT, GRAD_AT, TERM_AT = 0, BLOCK, 2 * BLOCK
QUERY_ROWS = TERM_AT + 16
KEY_AT, VALUE_AT = QUERY_ROWS, QUERY_ROWS + BLOCK
PACK_ROWS = QUERY_ROWS + 2 * BLOCK
INTERPRET = False


def nt(lhs, rhs):
    return lax.dot_general(
        lhs, rhs, (((1,), (1,)), ((), ())), preferred_element_type=jnp.float32
    )


def nn(lhs, rhs):
    return lax.dot_general(
        lhs, rhs, (((1,), (0,)), ((), ())), preferred_element_type=jnp.float32
    )


def tn(lhs, rhs):
    return lax.dot_general(
        lhs, rhs, (((0,), (0,)), ((), ())), preferred_element_type=jnp.float32
    )


def three_terms(value):
    high = value.astype(jnp.bfloat16).astype(jnp.float32)
    middle = (value - high).astype(jnp.bfloat16).astype(jnp.float32)
    return [high, middle, value - high - middle]


def norm_and_delta(rows):
    rows = rows.astype(jnp.float32)
    return rows[0:1] + rows[1:2] + rows[2:3], rows[3:4] + rows[4:5] + rows[5:6]


def pack_body(go_ref, o_ref, q_ref, norm_ref, own_ref, spread_ref, norm_buf, sems):
    def send(part, source, at):
        rows = pl.ds(at, source.shape[0])
        return [
            pltpu.make_async_copy(source, spread_ref.at[peer, rows], sems.at[part * RING + peer])
            for peer in range(RING)
        ]

    load = pltpu.make_async_copy(norm_ref, norm_buf, sems.at[3 * RING])
    load.start()
    copies = send(0, q_ref, QUERY_AT) + send(1, go_ref, GRAD_AT)
    for copy in copies:
        copy.start()
    own_ref[QUERY_AT:GRAD_AT] = q_ref[...]
    own_ref[GRAD_AT:TERM_AT] = go_ref[...]
    ones = jnp.ones((8, HEAD_DIM), jnp.float32)
    product = go_ref[...].astype(jnp.float32) * o_ref[...].astype(jnp.float32)
    deltas = []
    for at in range(0, go_ref.shape[1], HEAD_DIM):
        sums = lax.dot_general(
            ones,
            product[:, at : at + HEAD_DIM],
            (((1,), (1,)), ((), ())),
            precision=lax.Precision.HIGHEST,
            preferred_element_type=jnp.float32,
        )
        deltas.append(sums[0:1])
    load.wait()
    norms = [norm_buf[head : head + 1, :] for head in range(norm_buf.shape[0])]
    terms = three_terms(jnp.concatenate(norms, axis=1)) + three_terms(jnp.concatenate(deltas, axis=1))
    pad = jnp.zeros((QUERY_ROWS - TERM_AT - len(terms), go_ref.shape[1]), jnp.float32)
    own_ref[TERM_AT:QUERY_ROWS] = jnp.concatenate(terms + [pad], axis=0).astype(jnp.bfloat16)
    last = send(2, own_ref.at[pl.ds(TERM_AT, QUERY_ROWS - TERM_AT)], TERM_AT)
    for copy in last:
        copy.start()
    for copy in copies + last:
        copy.wait()


def key_side(keys, values, queries, grads, norms, deltas):
    weights = jnp.exp(nt(keys, queries) * SCALE - norms)
    dscores = weights * (nt(values, grads) - deltas)
    dscores_low = dscores.astype(jnp.bfloat16)
    grad_k = nn(dscores_low, queries) * SCALE
    grad_v = nn(weights.astype(jnp.bfloat16), grads)
    return grad_k, grad_v, dscores_low


def gathered(packs, cols):
    def rows(at):
        return jnp.concatenate([pack[at : at + BLOCK, cols] for pack in packs], axis=0)

    stats = [norm_and_delta(pack[TERM_AT:QUERY_ROWS, cols]) for pack in packs]
    norms, deltas = (jnp.concatenate(part, axis=1) for part in zip(*stats))
    return rows(QUERY_AT), rows(GRAD_AT), norms, deltas


def glob_body(place_ref, group_ref, gk_ref, gv_ref, out_ref):
    pieces = out_ref.shape[0]
    share = GLOB // RING
    share_at = pl.multiple_of(place_ref[0] * share, share)
    rows_each = share // pieces
    packs = [group_ref.at[member] for member in range(RING)]
    for head in range(gk_ref.shape[1] // HEAD_DIM):
        cols = slice(head * HEAD_DIM, (head + 1) * HEAD_DIM)
        grad_k, grad_v, _ = key_side(
            gk_ref[pl.ds(share_at, share), cols],
            gv_ref[pl.ds(share_at, share), cols],
            *gathered(packs, cols),
        )
        for piece in range(pieces):
            part = slice(piece * rows_each, (piece + 1) * rows_each)
            out_ref[piece, :, cols] = jnp.concatenate([grad_k[part], grad_v[part]], axis=0).astype(
                jnp.bfloat16
            )


def query_side(keys, values, queries, grads, norms, deltas):
    weights = jnp.exp(nt(keys, queries) * SCALE - norms)
    dscores = weights * (nt(values, grads) - deltas)
    return tn(dscores.astype(jnp.bfloat16), keys) * SCALE


def pair_body(k_ref, v_ref, out_ref):
    out_ref[0:BLOCK] = k_ref[...]
    out_ref[BLOCK:] = v_ref[...]


def whole_body(own_ref, k_ref, v_ref, before_ref, pack_ref):
    del before_ref
    pack_ref[0:QUERY_ROWS] = own_ref[...]
    pack_ref[KEY_AT:VALUE_AT] = k_ref[...]
    pack_ref[VALUE_AT:] = v_ref[...]


def own_body(pack_ref, before_ref, gk_ref, gv_ref, dq_ref, copy_ref):
    copy_ref[...] = pack_ref[...]
    for head in range(gk_ref.shape[1] // HEAD_DIM):
        cols = slice(head * HEAD_DIM, (head + 1) * HEAD_DIM)
        keys = jnp.concatenate(
            [pack_ref[KEY_AT:VALUE_AT, cols], before_ref[0:BLOCK, cols], gk_ref[:, cols]], axis=0
        )
        values = jnp.concatenate(
            [pack_ref[VALUE_AT:, cols], before_ref[BLOCK:, cols], gv_ref[:, cols]], axis=0
        )
        dq_ref[:, cols] = query_side(keys, values, *gathered([pack_ref], cols))


def far_body(
    place_ref, group_ref, pack_ref, far2_ref, far3_ref, dk_ref, dv_ref
):
    packs = [group_ref.at[lax.rem(place_ref[0] + hop, RING)] for hop in (2, 3, 1)]
    for head in range(dk_ref.shape[1] // HEAD_DIM):
        cols = slice(head * HEAD_DIM, (head + 1) * HEAD_DIM)
        own_k, own_v = pack_ref[KEY_AT:VALUE_AT, cols], pack_ref[VALUE_AT:, cols]
        grad_k, grad_v, dscores_low = key_side(own_k, own_v, *gathered(packs, cols))
        dk_ref[:, cols] = grad_k
        dv_ref[:, cols] = grad_v
        far_dq = (tn(dscores_low[:, 0 : 2 * BLOCK], own_k) * SCALE).astype(jnp.bfloat16)
        far2_ref[:, cols] = far_dq[0:BLOCK]
        far3_ref[:, cols] = far_dq[BLOCK:]


def near_body(
    pack_ref, left_ref, right_ref, own_dq_ref, far_dk_ref, far_dv_ref, dq_ref, dk_ref, dv_ref
):
    packs = [pack_ref, left_ref, right_ref]
    for head in range(dq_ref.shape[1] // HEAD_DIM):
        cols = slice(head * HEAD_DIM, (head + 1) * HEAD_DIM)
        queries, grads, norms, deltas = gathered(packs, cols)
        keys = jnp.concatenate([ref[KEY_AT:VALUE_AT, cols] for ref in packs[1:]], axis=0)
        values = jnp.concatenate([ref[VALUE_AT:, cols] for ref in packs[1:]], axis=0)
        dq_ref[:, cols] = own_dq_ref[:, cols] + query_side(
            keys, values, queries[0:BLOCK], grads[0:BLOCK], norms[:, 0:BLOCK], deltas[:, 0:BLOCK]
        )
        grad_k, grad_v, _ = key_side(
            pack_ref[KEY_AT:VALUE_AT, cols], pack_ref[VALUE_AT:, cols], queries, grads, norms, deltas
        )
        dk_ref[:, cols] = (far_dk_ref[:, cols] + grad_k).astype(jnp.bfloat16)
        dv_ref[:, cols] = (far_dv_ref[:, cols] + grad_v).astype(jnp.bfloat16)


def finish_body(dq_ref, far2_ref, far3_ref, terms_ref, out_ref, gk_ref, gv_ref):
    total = dq_ref[...]
    for ref in (far2_ref, far3_ref):
        total = total + ref[...].astype(jnp.float32)
    out_ref[...] = total.astype(jnp.bfloat16)
    terms = jnp.sum(terms_ref[...].astype(jnp.float32), axis=0)
    rows = gk_ref.shape[0]
    gk_ref[...] = terms[0:rows]
    gv_ref[...] = terms[rows:]


def in_vmem(count):
    return [pl.BlockSpec(memory_space=pltpu.VMEM) for _ in range(count)]


def near(value):
    return pltpu.with_memory_space_constraint(value, pltpu.VMEM)


def shards(queries, keys, values, outputs, grad_out, log_norm, glob_keys, glob_values, key_lists):
    cols = queries.shape[1]
    z_count = lax.axis_size("z")
    peers = lax.axis_size("head")
    ctx_count = RING * z_count
    share_rows = GLOB // ctx_count
    bf16, f32 = jnp.bfloat16, jnp.float32
    shape = jax.ShapeDtypeStruct
    place_spec = pl.BlockSpec(memory_space=pltpu.SMEM)
    place = lax.axis_index("x").astype(jnp.int32).reshape(1)

    def beside(value, by):
        pairs = [(i, i + by) for i in range(ctx_count) if 0 <= i + by < ctx_count]
        return lax.ppermute(value, ("x", "z"), pairs)

    def back(value, hop):
        pairs = [(i, (i + hop * z_count) % ctx_count) for i in range(ctx_count)]
        return lax.ppermute(value, ("x", "z"), pairs)

    def swap(value, axis):
        return lax.all_to_all(value, axis, split_axis=0, concat_axis=0, tiled=True)

    split = grad_out.reshape(BLOCK // peers, peers, cols).transpose(1, 0, 2)
    incoming = swap(split, "head").reshape(BLOCK, cols)
    pair = pl.pallas_call(
        pair_body,
        out_shape=pltpu.VMEM((2 * BLOCK, cols), bf16),
        in_specs=in_vmem(2),
        out_specs=in_vmem(1)[0],
        interpret=INTERPRET,
        name="pair",
    )(keys, values)
    before = near(back(pair, 1))
    own_rows, spread = pl.pallas_call(
        pack_body,
        out_shape=(
            pltpu.VMEM((QUERY_ROWS, cols), bf16),
            shape((RING, QUERY_ROWS, cols), bf16),
        ),
        in_specs=in_vmem(3) + [pl.BlockSpec(memory_space=pl.ANY)],
        out_specs=[pl.BlockSpec(memory_space=pltpu.VMEM), pl.BlockSpec(memory_space=pl.ANY)],
        scratch_shapes=[
            pltpu.VMEM(log_norm.shape, f32),
            pltpu.SemaphoreType.DMA((3 * RING + 1,)),
        ],
        interpret=INTERPRET,
        cost_estimate=pl.CostEstimate(flops=1000000000, transcendentals=0, bytes_accessed=0),
        name="pack",
    )(near(incoming), near(outputs), near(queries), log_norm)
    group = near(swap(spread, "x"))
    gk_near, gv_near = near(glob_keys), near(glob_values)
    pack = pl.pallas_call(
        whole_body,
        out_shape=pltpu.VMEM((PACK_ROWS, cols), bf16),
        in_specs=in_vmem(4),
        out_specs=in_vmem(1)[0],
        interpret=INTERPRET,
        cost_estimate=pl.CostEstimate(flops=5000000000, transcendentals=0, bytes_accessed=0),
        name="whole_pack",
    )(near(own_rows), near(keys), near(values), before)
    right = near(beside(pack, -1))
    own_dq, pack_copy = pl.pallas_call(
        own_body,
        out_shape=(pltpu.VMEM((BLOCK, cols), f32), pltpu.VMEM((PACK_ROWS, cols), bf16)),
        in_specs=in_vmem(4),
        out_specs=in_vmem(2),
        interpret=INTERPRET,
        name="own_grads",
    )(near(pack), before, gk_near, gv_near)
    left = near(beside(pack_copy, 1))
    glob = pl.pallas_call(
        glob_body,
        out_shape=pltpu.VMEM((z_count, 2 * share_rows, cols), bf16),
        in_specs=[place_spec] + in_vmem(3),
        out_specs=in_vmem(1)[0],
        interpret=INTERPRET,
        name="glob_grads",
    )(place, group, gk_near, gv_near)
    terms = near(swap(glob, "z"))
    *far, far_dk, far_dv = pl.pallas_call(
        far_body,
        out_shape=(
            pltpu.VMEM((BLOCK, cols), bf16),
            pltpu.VMEM((BLOCK, cols), bf16),
            pltpu.VMEM((BLOCK, cols), f32),
            pltpu.VMEM((BLOCK, cols), f32),
        ),
        in_specs=[place_spec] + in_vmem(2),
        out_specs=in_vmem(4),
        interpret=INTERPRET,
        name="far_grads",
    )(place, group, near(pack))
    far = [near(back(part, hop)) for part, hop in zip(far, (2, 3))]
    dq, dk, dv = pl.pallas_call(
        near_body,
        out_shape=(
            pltpu.VMEM((BLOCK, cols), f32),
            shape((BLOCK, cols), bf16),
            shape((BLOCK, cols), bf16),
        ),
        in_specs=in_vmem(6),
        out_specs=in_vmem(3),
        interpret=INTERPRET,
        name="near_grads",
    )(near(pack), left, right, near(own_dq), near(far_dk), near(far_dv))
    dq, gk, gv = pl.pallas_call(
        finish_body,
        out_shape=(
            shape((BLOCK, cols), bf16),
            shape((share_rows, cols), f32),
            shape((share_rows, cols), f32),
        ),
        in_specs=in_vmem(4),
        out_specs=in_vmem(3),
        interpret=INTERPRET,
        name="finish",
    )(near(dq), *far, terms)
    return dq, dk, dv, gk, gv


def solution(mesh):
    ctx_count, head_count = mesh.shape["ctx"], mesh.shape["head"]
    grid = Mesh(
        mesh.devices.reshape(RING, ctx_count // RING, head_count), ("x", "z", "head")
    )
    ctx = ("x", "z")
    in_specs = (
        P(ctx, "head"),
        P(ctx, "head"),
        P(ctx, "head"),
        P(ctx, "head"),
        P((*ctx, "head"), None),
        P("head", ctx),
        P(None, "head"),
        P(None, "head"),
        P(),
    )
    out_specs = (P(ctx, "head"),) * 5
    return jax.shard_map(shards, mesh=grid, in_specs=in_specs, out_specs=out_specs, check_vma=False)
```
